512 devices in a mesh: dom: 32 (over x, z), slab: 16 (over y, core).
Axes of the slice: x: 4, y: 8, z: 8, core: 2. Of those that a mesh axis runs over, the one named last changes fastest.
Arguments:
- equivariant_embedding: bfloat16 [32, 16, 128, 25, 128], P('dom', 'slab'), may hold values from -6 to 6
- cartesian_coordinates: float32 [32, 16, 3, 128], P('dom', 'slab'), may hold values from 0 to 40
- element_identity: int32 [32, 16, 128], P('dom', 'slab'), may hold values from 0 to 3
- occupied_site_totals: int32 [32, 16], P('dom', 'slab'), may hold values from 32 to 128, as said below
- halo_export_indices: int32 [32, 16, 32], P('dom', 'slab'), may hold values from 0 to 127, as said below
- adjacency_rows: int32 [32, 16, 128, 64], P('dom', 'slab'), may hold values from -1 to 415, as said below
- attention_source_weights: bfloat16 [128, 128], replicated, may hold values from -0.5 to 0.5
- attention_target_weights: bfloat16 [128, 128], replicated, may hold values from -0.5 to 0.5
- degree_channel_mixer: bfloat16 [5, 128, 128], replicated, may hold values from -0.5 to 0.5
- affinity_output_head: float32 [5, 128], replicated, may hold values from -0.25 to 0.25
- baseline_affinity_per_element: float32 [4], replicated, may hold values from -3 to 3
- chemical_stiffness: float32 [4], replicated, may hold values from 2 to 5
- reciprocal_lattice_points: float32 [3, 4096], replicated, may hold values from -1 to 1
- ewald_weighting: float32 [4096], replicated, may hold values from 0.005 to 0.05
Outputs:
- charges: float32 [32, 16, 128], P('dom', 'slab')
- forces: float32 [32, 16, 3, 128], P('dom', 'slab')
The draws below stay inside these ranges and needn't reach their ends.
Inputs may be any that keep to these rules, and one draw needn't show every extreme that they name: `occupied_site_totals`: live atoms occupy the slots below a device's count; the count of at least one device is 128. `halo_export_indices`: every entry is a live slot of its own device, below that device's occupied_site_totals. `adjacency_rows`: entries -1 are empty; an atom's filled entries come first, are distinct, name live own slots or ghost rows, never the middle block (3a+b = 4); slots that are not live have only -1; every live atom has at least 16 filled entries and some atom of every device has 64.
All inputs are finite; a program needn't handle non-finite values.
Results may differ from the reference program's by a relative error of at most 0.0021.
Values may be sent and summed in bfloat16 or wider, within the bound.
A program may use at most 64 MiB of HBM per device.

```python
import math
import jax
import jax.numpy as jnp
from jax import lax

CH = 128
LMAX = 4
RECIP_KPOINTS = 4096
NBR = 64
ELEMENTS = 4
ITERS = 4
ATOMS_DEV = 128
GHOSTS = 32
COMPS = 25
DOMAINS = 32
SLABS = 16
ATOMS_ALL = 65536


def live_counts(key):
    quarter = ATOMS_DEV // 4
    counts = jax.random.randint(jax.random.fold_in(key, 11), (DOMAINS, SLABS), quarter, quarter + 3 * ATOMS_DEV // 8 + 1, dtype=jnp.int32)
    chosen = jax.random.randint(jax.random.fold_in(key, 12), (), 0, DOMAINS * SLABS, dtype=jnp.int32)
    flat_counts = counts.reshape(-1)
    flat_counts = jnp.where(jnp.arange(DOMAINS * SLABS, dtype=jnp.int32) == chosen, ATOMS_DEV, flat_counts)
    return flat_counts.reshape(DOMAINS, SLABS).astype(jnp.int32)


def draw_occupied_site_totals(key, part):
    return live_counts(key)


def draw_halo_export_indices(key, part):
    counts = live_counts(key)
    raw_draw = jax.random.randint(jax.random.fold_in(key, 21), (DOMAINS, SLABS, GHOSTS), 0, 1 << 30, dtype=jnp.int32)
    return (raw_draw % counts[:, :, None]).astype(jnp.int32)


def draw_adjacency_rows(key, part):
    counts = live_counts(key)[:, :, None, None]
    full_shape = (DOMAINS, SLABS, ATOMS_DEV, NBR)
    span_all = counts + 8 * GHOSTS
    bucket = span_all // NBR
    start_draw = jax.random.randint(jax.random.fold_in(key, 31), (DOMAINS, SLABS, ATOMS_DEV, 1), 0, 1 << 30, dtype=jnp.int32) % span_all
    jitter = jax.random.randint(jax.random.fold_in(key, 32), full_shape, 0, 1 << 30, dtype=jnp.int32) % bucket
    slot_index = jnp.arange(NBR, dtype=jnp.int32)[None, None, None, :]
    picked = (start_draw + slot_index * bucket + jitter) % span_all
    ghost_part = jnp.maximum(picked - counts, 0)
    ghost_block = ghost_part // GHOSTS
    ghost_block = ghost_block + (ghost_block >= 4).astype(jnp.int32)
    table_index = jnp.where(picked < counts, picked, ATOMS_DEV + ghost_block * GHOSTS + ghost_part % GHOSTS)
    entry_count = jax.random.randint(jax.random.fold_in(key, 33), (DOMAINS, SLABS, ATOMS_DEV, 1), NBR // 4, NBR + 1, dtype=jnp.int32)
    full_atom = jax.random.randint(jax.random.fold_in(key, 34), (DOMAINS, SLABS, 1, 1), 0, 1 << 30, dtype=jnp.int32) % counts
    atom_index = jnp.arange(ATOMS_DEV, dtype=jnp.int32)[None, None, :, None]
    entry_count = jnp.where(atom_index == full_atom, NBR, entry_count)
    filled = (atom_index < counts) & (slot_index < entry_count)
    return jnp.where(filled, table_index, -1).astype(jnp.int32)


def plant(result, key, low, high):
    shape = result.shape
    place = [jax.random.randint(jax.random.fold_in(key, axis), (), 0, shape[axis]) for axis in range(len(shape))]
    result = result.at[tuple(place)].set(low)
    longest = shape.index(max(shape))
    place[longest] = (place[longest] + 1) % shape[longest]
    return result.at[tuple(place)].set(high)


def levels(stream_key, shape, shards, smallest, top_value):
    loudness, own = 1.0, jax.random.fold_in(stream_key, 6)
    for position, parts in shards:
        heights = jnp.exp(jax.random.uniform(jax.random.fold_in(own, position), (parts,), jnp.float32, smallest / len(shards), top_value / len(shards)))
        loudness = loudness * jnp.repeat(heights, shape[position] // parts).reshape([-1 if axis == position else 1 for axis in range(len(shape))])
    return loudness


def centred(stream_key, extent, deviation, limit, shards=(), kind=jnp.bfloat16):
    gain = levels(stream_key, extent, shards, -0.22, 0.18) if shards else 1.0
    values = jax.random.normal(stream_key, extent, jnp.float32) * deviation * gain
    return jnp.minimum(jnp.maximum(values, -limit), limit).astype(kind)


def setup_inputs(seed: int = 0) -> dict:
    arg_keys = jax.random.split(jax.random.key(seed), 15)
    equivariant_embedding = centred(arg_keys[0], (DOMAINS, SLABS, ATOMS_DEV, COMPS, CH), 1.0, 6.0, ((0, 32), (1, 16)))
    cartesian_coordinates = jnp.clip(40.0 * jax.random.uniform(arg_keys[1], (DOMAINS, SLABS, 3, ATOMS_DEV), jnp.float32) ** levels(arg_keys[1], (DOMAINS, SLABS, 3, ATOMS_DEV), ((0, 32), (1, 16)), -0.2, 0.2), 0.0, 40.0)
    element_identity = plant(jax.random.randint(arg_keys[2], (DOMAINS, SLABS, ATOMS_DEV), 0, ELEMENTS), jax.random.fold_in(arg_keys[2], 1), 0, ELEMENTS - 1).astype(jnp.int32)
    occupied_site_totals = draw_occupied_site_totals(jax.random.fold_in(arg_keys[14], 71), 0)
    halo_export_indices = draw_halo_export_indices(jax.random.fold_in(arg_keys[14], 71), 0)
    adjacency_rows = draw_adjacency_rows(jax.random.fold_in(arg_keys[14], 71), 0)
    attention_source_weights = centred(arg_keys[6], (CH, CH), CH ** -0.5, 0.5)
    attention_target_weights = centred(arg_keys[7], (CH, CH), CH ** -0.5, 0.5)
    degree_channel_mixer = centred(arg_keys[8], (LMAX + 1, CH, CH), CH ** -0.5, 0.5)
    affinity_output_head = centred(arg_keys[9], (LMAX + 1, CH), ((LMAX + 1) * CH) ** -0.5, 0.25, (), jnp.float32)
    baseline_affinity_per_element = centred(arg_keys[10], (ELEMENTS,), 1.0, 3.0, (), jnp.float32)
    chemical_stiffness = jnp.clip(jax.random.uniform(arg_keys[11], (ELEMENTS,), jnp.float32, 2.0, 5.0), 2.0, 5.0)
    reciprocal_lattice_points = jnp.clip(jax.random.uniform(arg_keys[12], (3, RECIP_KPOINTS), jnp.float32, -1.0, 1.0), -1.0, 1.0)
    ewald_weighting = jnp.clip(jnp.exp(jax.random.uniform(arg_keys[13], (RECIP_KPOINTS,), jnp.float32, math.log(0.005), math.log(0.05))), 0.005, 0.05)
    return {"equivariant_embedding": equivariant_embedding, "cartesian_coordinates": cartesian_coordinates, "element_identity": element_identity, "occupied_site_totals": occupied_site_totals, "halo_export_indices": halo_export_indices, "adjacency_rows": adjacency_rows, "attention_source_weights": attention_source_weights, "attention_target_weights": attention_target_weights, "degree_channel_mixer": degree_channel_mixer, "affinity_output_head": affinity_output_head, "baseline_affinity_per_element": baseline_affinity_per_element, "chemical_stiffness": chemical_stiffness, "reciprocal_lattice_points": reciprocal_lattice_points, "ewald_weighting": ewald_weighting}


highest_accuracy_mode = lax.Precision.HIGHEST

def project_values(row_block, degree_channel_mixer):
    pieces = []
    for degree in range(degree_channel_mixer.shape[0]):
        first_comp = degree * degree
        last_comp = (degree + 1) * (degree + 1)
        product_part = jnp.einsum('ncd,de->nce', row_block[:, first_comp:last_comp, :].astype(jnp.float32), degree_channel_mixer[degree].astype(jnp.float32))
        pieces.append(product_part.astype(jnp.bfloat16))
    joined = jnp.concatenate(pieces, axis=1)
    return joined.reshape(row_block.shape[0], -1)

def readout_sum(message, affinity_output_head):
    result_sum = lax.optimization_barrier(jnp.sum(message[:, 0, :] * affinity_output_head[0], axis=1))
    for degree in range(1, affinity_output_head.shape[0]):
        first_comp = degree * degree
        last_comp = (degree + 1) * (degree + 1)
        part_sq = message[:, first_comp:last_comp, :] * message[:, first_comp:last_comp, :]
        channel_norm = jnp.sqrt(lax.optimization_barrier(jnp.sum(part_sq, axis=1)) + 1e-06)
        result_sum = result_sum + lax.optimization_barrier(jnp.sum(channel_norm * affinity_output_head[degree], axis=1))
    return result_sum

def reciprocal_angles(shard_layout, reciprocal_lattice_points):
    initial_addend = shard_layout[0][:, None] * reciprocal_lattice_points[0][None, :]
    central_addend = shard_layout[1][:, None] * reciprocal_lattice_points[1][None, :]
    final_addend = shard_layout[2][:, None] * reciprocal_lattice_points[2][None, :]
    return initial_addend + central_addend + final_addend

def reference(equivariant_embedding, cartesian_coordinates, element_identity, occupied_site_totals, halo_export_indices, adjacency_rows, attention_source_weights, attention_target_weights, degree_channel_mixer, affinity_output_head, baseline_affinity_per_element, chemical_stiffness, reciprocal_lattice_points, ewald_weighting):
    devices_all = DOMAINS * SLABS
    feats_flat = equivariant_embedding.reshape(devices_all, ATOMS_DEV, COMPS, CH)

    def local_rows(feat_dev):
        scalar_ch = feat_dev[:, 0, :]
        query_rows = jnp.dot(scalar_ch, attention_source_weights, preferred_element_type=jnp.float32).astype(jnp.bfloat16)
        key_rows = jnp.dot(scalar_ch, attention_target_weights, preferred_element_type=jnp.float32).astype(jnp.bfloat16)
        value_rows = project_values(feat_dev, degree_channel_mixer)
        return (query_rows, key_rows, value_rows)
    queries, key_rows, value_rows = lax.map(local_rows, feats_flat)
    key_flat = key_rows.reshape(devices_all * ATOMS_DEV, CH)
    value_flat = value_rows.reshape(devices_all * ATOMS_DEV, COMPS * CH)
    send_flat = halo_export_indices.reshape(devices_all, GHOSTS)
    neigh_flat = adjacency_rows.reshape(devices_all, ATOMS_DEV, NBR)
    species_flat = element_identity.reshape(devices_all, ATOMS_DEV)
    offsets = jnp.arange(9, dtype=jnp.int32)

    def electro_dev(device):
        dom_index = device // SLABS
        slab_index = device % SLABS
        source = (dom_index + offsets // 3 - 1) % DOMAINS * SLABS + (slab_index + offsets % 3 - 1) % SLABS
        ghost_rows = source[:, None] * ATOMS_DEV + send_flat[source]
        own_rows = device * ATOMS_DEV + jnp.arange(ATOMS_DEV, dtype=jnp.int32)
        table_rows = jnp.concatenate([own_rows, ghost_rows.reshape(-1)]).astype(jnp.int32)
        neigh_dev = neigh_flat[device]
        valid_slot = neigh_dev >= 0
        global_rows = table_rows[jnp.maximum(neigh_dev, 0)]
        scores = jnp.einsum('ac,anc->an', queries[device].astype(jnp.float32), key_flat[global_rows].astype(jnp.float32))
        weights = jnp.where(valid_slot, jax.nn.sigmoid(scores / math.sqrt(CH)) * 0.125, 0.0).astype(jnp.bfloat16)
        message = jnp.einsum('an,anc->ac', weights.astype(jnp.float32), value_flat[global_rows].astype(jnp.float32))
        message = message.reshape(ATOMS_DEV, COMPS, CH)
        return readout_sum(message, affinity_output_head) + baseline_affinity_per_element[species_flat[device]]
    electroneg = lax.map(electro_dev, jnp.arange(devices_all, dtype=jnp.int32))
    live_slots = jnp.arange(ATOMS_DEV, dtype=jnp.int32)[None, :] < occupied_site_totals.reshape(devices_all, 1)
    rhs_vec = jnp.where(live_slots, -electroneg, 0.0)
    hard_diag = chemical_stiffness[species_flat]
    place_flat = cartesian_coordinates.reshape(devices_all, 3, ATOMS_DEV)
    recip_scale = 1.0 / math.sqrt(ATOMS_ALL)

    def factors(vector_in):

        def scan_step(running, scan_item):
            shard_layout, vector_dev = scan_item
            angle_table_fetch = reciprocal_angles(shard_layout, reciprocal_lattice_points)
            cos_part = jnp.dot(vector_dev, jnp.cos(angle_table_fetch), precision=highest_accuracy_mode)
            sin_part = jnp.dot(vector_dev, jnp.sin(angle_table_fetch), precision=highest_accuracy_mode)
            return ((running[0] + cos_part, running[1] + sin_part), None)
        start_pair = (jnp.zeros((RECIP_KPOINTS,), jnp.float32), jnp.zeros((RECIP_KPOINTS,), jnp.float32))
        summed, unused = lax.scan(scan_step, start_pair, (place_flat, vector_in))
        return summed

    def operator(vector_in):
        cos_sum, sin_sum = factors(vector_in)

        def back_dev(shard_layout):
            angle_table_fetch = reciprocal_angles(shard_layout, reciprocal_lattice_points)
            return jnp.dot(jnp.cos(angle_table_fetch), ewald_weighting * cos_sum, precision=highest_accuracy_mode) + jnp.dot(jnp.sin(angle_table_fetch), ewald_weighting * sin_sum, precision=highest_accuracy_mode)
        recip_part = lax.map(back_dev, place_flat)
        return jnp.where(live_slots, hard_diag * vector_in + recip_scale * recip_part, 0.0)
    charges = jnp.zeros_like(rhs_vec)
    residual = rhs_vec
    direction = rhs_vec
    resid_norm = jnp.sum(residual * residual)
    for iteration in range(ITERS):
        image_vec = operator(direction)
        step_size = resid_norm / jnp.sum(direction * image_vec)
        charges = charges + step_size * direction
        residual = residual - step_size * image_vec
        norm_next = jnp.sum(residual * residual)
        direction = residual + norm_next / resid_norm * direction
        resid_norm = norm_next
    structure_factor_real, structure_factor_imag = factors(charges)

    def field_dev(shard_layout):
        angle_table_fetch = reciprocal_angles(shard_layout, reciprocal_lattice_points)
        odd_part_result = jnp.dot(jnp.sin(angle_table_fetch), (ewald_weighting * structure_factor_real)[:, None] * reciprocal_lattice_points.T, precision=highest_accuracy_mode)
        even_part_result = jnp.dot(jnp.cos(angle_table_fetch), (ewald_weighting * structure_factor_imag)[:, None] * reciprocal_lattice_points.T, precision=highest_accuracy_mode)
        return recip_scale * (odd_part_result - even_part_result)
    efield_rows = lax.map(field_dev, place_flat)
    forces = charges[:, :, None] * efield_rows
    forces = jnp.transpose(forces, (0, 2, 1)).reshape(DOMAINS, SLABS, 3, ATOMS_DEV)
    return (charges.reshape(DOMAINS, SLABS, ATOMS_DEV), forces)
```

```python
import math

import jax
import jax.numpy as jnp
from jax import lax
from jax.experimental import pallas as pl
from jax.experimental.pallas import tpu as pltpu
from jax.sharding import PartitionSpec as P

ITERS = 4
CHIPS_X = 4
LANES = 128
MESH = pl.DeviceIdType.MESH
F32 = jnp.float32

HALF_PI_PARTS = (1.5703125, 4.837512969970703125e-4, 7.54978995489188216e-8)


def sine_cosine(phase):
    quadrant = jnp.round(phase * (2.0 / math.pi))
    reduced = phase - quadrant * HALF_PI_PARTS[0]
    reduced = reduced - quadrant * HALF_PI_PARTS[1]
    reduced = reduced - quadrant * HALF_PI_PARTS[2]
    square = reduced * reduced
    odd = (-1.9515295891e-4 * square + 8.3321608736e-3) * square - 1.6666654611e-1
    odd = odd * square * reduced + reduced
    even = (2.443315711809948e-5 * square - 1.388731625493765e-3) * square
    even = (even + 4.166664568298827e-2) * square * square - 0.5 * square + 1.0
    turn = quadrant.astype(jnp.int32)
    swap = (turn & 1) == 1
    sine = jnp.where(swap, even, odd)
    cosine = jnp.where(swap, odd, even)
    sine = jnp.where((turn & 2) == 2, -sine, sine)
    cosine = jnp.where(((turn + 1) & 2) == 2, -cosine, cosine)
    return sine, cosine


def lines(shape):
    chips_x, chips_y, chips_z = shape
    dom, slab = lax.axis_index("dom"), lax.axis_index("slab")
    x, z = dom // chips_z, dom % chips_z
    y, core = slab // 2, slab % 2

    def place(px, py, pz, pc):
        return (px * chips_z + pz, py * 2 + pc)

    ring = chips_y
    along = [
        place(x, (y + j * (1 - core)) % chips_y, (z + j * core) % chips_z, core)
        for j in range(1, ring)
    ]
    across = [
        place(x, (y + j * core) % chips_y, (z + j * (1 - core)) % chips_z, core)
        for j in range(1, ring)
    ]
    pair = place(x, y, z, 1 - core)
    last = [
        place((x + i // 2) % chips_x, y, z, (core + i % 2) % 2) for i in range(1, 2 * chips_x)
    ]
    return core, pair, along, across, last


def row_of(column, eye):
    return jnp.sum(jnp.where(eye, column, 0.0), axis=0, keepdims=True)


def column_of(row, eye):
    wide = jnp.broadcast_to(row, (LANES, LANES))
    return jnp.broadcast_to(
        jnp.sum(jnp.where(eye, wide, 0.0), axis=1, keepdims=True), (LANES, LANES)
    )


def identity_mask():
    return lax.broadcasted_iota(jnp.int32, (LANES, LANES), 0) == lax.broadcasted_iota(
        jnp.int32, (LANES, LANES), 1
    )


def fill_tables(place_ref, waves_ref, sites, cos_ref, sin_ref, eye):
    for axis in range(3):
        sites[axis] = column_of(place_ref[axis], eye)
    step_rows = 32

    def per_block(block, carry):
        lanes = pl.ds(pl.multiple_of(block * LANES, LANES), LANES)

        def per_rows(part, inner):
            rows = pl.ds(pl.multiple_of(part * step_rows, step_rows), step_rows)
            phase = (
                sites[0, rows, :] * waves_ref[0:1, lanes]
                + sites[1, rows, :] * waves_ref[1:2, lanes]
                + sites[2, rows, :] * waves_ref[2:3, lanes]
            )
            sine, cosine = sine_cosine(phase)
            cos_ref[block, rows, :] = cosine
            sin_ref[block, rows, :] = sine
            return inner

        return lax.fori_loop(0, LANES // step_rows, per_rows, carry)

    lax.fori_loop(0, cos_ref.shape[0], per_block, 0)


def cg_kernel(
    shape,
    negative_ref,
    species_ref,
    count_ref,
    place_ref,
    stiffness_ref,
    waves_ref,
    weight_ref,
    charges_ref,
    forces_ref,
    cos_ref,
    sin_ref,
    sites,
    vectors,
    mine,
    parts,
    total,
    whole,
    weighted,
    inbox,
    send_sem,
    recv_sem,
):
    core, pair, along, across, last = lines(shape)
    everyone = along + across + last
    barrier = pltpu.get_barrier_semaphore()
    for partner in everyone:
        pl.semaphore_signal(barrier, inc=1, device_id=partner, device_id_type=MESH)

    blocks = cos_ref.shape[0]
    scale = 1.0 / math.sqrt(lax.axis_size("dom") * lax.axis_size("slab") * LANES)
    eye = identity_mask()
    fill_tables(place_ref, waves_ref, sites, cos_ref, sin_ref, eye)

    species = species_ref[...]
    hardness = jnp.zeros(species.shape, F32)
    for element in range(stiffness_ref.shape[0]):
        hardness = jnp.where(species == element, stiffness_ref[element], hardness)
    slots = lax.broadcasted_iota(jnp.int32, (1, LANES), 1)
    live = slots < count_ref[0, 0]
    vectors[0] = column_of(jnp.where(live, negative_ref[...], 0.0), eye)
    vectors[1] = jnp.zeros((LANES, LANES), F32)
    vectors[2] = jnp.zeros((LANES, LANES), F32)
    vectors[3] = column_of(hardness, eye)
    vectors[4] = column_of(jnp.where(live, 1.0, 0.0), eye)
    mine[...] = jnp.zeros_like(mine)
    total[...] = jnp.zeros_like(total)

    pl.semaphore_wait(barrier, len(everyone))

    stages = ([pair], along, across, last)

    def copy(turn, number, source, target):
        return pltpu.make_async_remote_copy(
            src_ref=source,
            dst_ref=inbox.at[turn, number],
            send_sem=send_sem.at[number],
            recv_sem=recv_sem.at[turn, number],
            device_id=target,
            device_id_type=MESH,
        )

    def global_sum(turn):
        started = []

        def stage(targets, source):
            base = len(started)
            now = [copy(turn, base + i, source, target) for i, target in enumerate(targets)]
            for item in now:
                item.start()
            started.extend(now)
            return base, now

        base, now = stage([pair], mine.at[1 - core])
        held = mine[core]
        now[0].wait_recv()
        held = held + inbox[turn, base]
        for number, targets in enumerate((along, across)):
            parts[number] = held
            base, now = stage(targets, parts.at[number])
            for i, item in enumerate(now):
                item.wait_recv()
                held = held + inbox[turn, base + i]
        parts[2] = held
        base, now = stage(last, parts.at[2])
        other = jnp.zeros_like(held)
        for i, item in enumerate(now):
            item.wait_recv()
            if (i + 1) % 2 == 0:
                held = held + inbox[turn, base + i]
            else:
                other = other + inbox[turn, base + i]
        for item in started:
            item.wait_send()
        even = core == 0
        whole[0] = jnp.where(even, held, other)
        whole[1] = jnp.where(even, other, held)

    def iteration(turn, carry):
        previous_norm, stiff_part = carry
        residual, hard = vectors[0], vectors[3]
        hard_residual = hard * residual

        def project(block, inner):
            row = pl.ds(block, 1)
            mine[0, row, :] = jnp.sum(cos_ref[block] * residual, axis=0, keepdims=True)
            mine[1, row, :] = jnp.sum(sin_ref[block] * residual, axis=0, keepdims=True)
            return inner

        lax.fori_loop(0, blocks, project, 0)
        scalars = (residual * residual, hard_residual * residual, hard_residual * vectors[1])
        for i, product in enumerate(scalars):
            mine[0, blocks + i : blocks + i + 1, :] = jnp.sum(product, axis=0, keepdims=True)
        global_sum(turn)
        norm = whole[0, blocks : blocks + 1, :]
        beta = jnp.where(turn > 0, norm / previous_norm, 0.0)
        stiff_part = (
            whole[0, blocks + 1 : blocks + 2, :]
            + 2.0 * beta * whole[0, blocks + 2 : blocks + 3, :]
            + beta * beta * stiff_part
        )
        weight = weight_ref[...]
        recip = jnp.zeros_like(weight)
        for part in range(2):
            factors = whole[part, 0:blocks, :] + beta * total[part, 0:blocks, :]
            total[part, 0:blocks, :] = factors
            weighted[part] = weight * factors
            recip = recip + weight * factors * factors
        recip = jnp.sum(jnp.sum(recip, axis=0, keepdims=True), axis=1, keepdims=True)
        step = norm / (stiff_part + scale * recip)
        direction = residual + beta * vectors[1]
        vectors[1] = direction

        def back(block, acc):
            row = pl.ds(block, 1)
            return acc + cos_ref[block] * weighted[0, row, :] + sin_ref[block] * weighted[1, row, :]

        image = lax.fori_loop(0, blocks, back, jnp.zeros((LANES, LANES), F32))
        image = hard * direction + scale * jnp.sum(image, axis=1, keepdims=True)
        image = vectors[4] * image
        vectors[2] = vectors[2] + step * direction
        vectors[0] = residual - step * image
        for part in range(2):
            total[2 + part] = total[2 + part] + step * weighted[part]
        return norm, stiff_part

    ones = jnp.ones((1, LANES), F32)
    lax.fori_loop(0, ITERS, iteration, (ones, ones))

    charges = vectors[2]
    charges_ref[...] = row_of(charges, eye)
    half = LANES // 2
    for part in range(2):
        rows = pl.ds(part * half, half)

        def field(block, acc):
            row = pl.ds(block, 1)
            lanes = pl.ds(pl.multiple_of(block * LANES, LANES), LANES)
            term = sin_ref[block, rows, :] * total[2, row, :] - cos_ref[block, rows, :] * total[3, row, :]
            return tuple(acc[axis] + term * waves_ref[axis : axis + 1, lanes] for axis in range(3))

        zero = jnp.zeros((half, LANES), F32)
        field_parts = lax.fori_loop(0, blocks, field, (zero, zero, zero))
        for axis in range(3):
            column = scale * jnp.sum(field_parts[axis], axis=1, keepdims=True)
            sites[axis, rows, :] = jnp.broadcast_to(column, (half, LANES))
    for axis in range(3):
        forces_ref[axis] = row_of(charges * sites[axis], eye)


def equilibrate(shape, negative, species, count, place, stiffness, waves, weight):
    blocks = waves.shape[1] // LANES
    chips_x, ring, _ = shape
    copies = 1 + 2 * (ring - 1) + 2 * chips_x - 1
    vmem = pl.BlockSpec(memory_space=pltpu.VMEM)
    smem = pl.BlockSpec(memory_space=pltpu.SMEM)
    return pl.pallas_call(
        lambda *refs: cg_kernel(shape, *refs),
        name="equilibrate",
        out_shape=(
            jax.ShapeDtypeStruct((1, LANES), F32),
            jax.ShapeDtypeStruct((3, 1, LANES), F32),
        ),
        in_specs=[vmem, vmem, smem, vmem, smem, vmem, vmem],
        out_specs=(vmem, vmem),
        scratch_shapes=[
            pltpu.VMEM((blocks, LANES, LANES), F32),
            pltpu.VMEM((blocks, LANES, LANES), F32),
            pltpu.VMEM((3, LANES, LANES), F32),
            pltpu.VMEM((5, LANES, LANES), F32),
            pltpu.VMEM((2, blocks + 8, LANES), F32),
            pltpu.VMEM((3, blocks + 8, LANES), F32),
            pltpu.VMEM((4, blocks, LANES), F32),
            pltpu.VMEM((2, blocks + 8, LANES), F32),
            pltpu.VMEM((2, blocks, LANES), F32),
            pltpu.VMEM((ITERS, copies, blocks + 8, LANES), F32),
            pltpu.SemaphoreType.DMA((copies,)),
            pltpu.SemaphoreType.DMA((ITERS, copies)),
        ],
        compiler_params=pltpu.CompilerParams(
            collective_id=1, has_side_effects=True, vmem_limit_bytes=48 * 1024 * 1024
        ),
    )(negative, species, count, place, stiffness, waves, weight.reshape(blocks, LANES))


def extended(cells, sides, width):
    for axis, dim in sides:
        count = lax.axis_size(axis)
        head = lax.slice_in_dim(cells, 0, width, axis=dim)
        tail = lax.slice_in_dim(cells, cells.shape[dim] - width, cells.shape[dim], axis=dim)
        cells = jnp.concatenate(
            [
                lax.ppermute(tail, axis, [(i, (i + 1) % count) for i in range(count)]),
                cells,
                lax.ppermute(head, axis, [((i + 1) % count, i) for i in range(count)]),
            ],
            axis=dim,
        )
    return cells


def project_values(row_block, degree_channel_mixer):
    pieces = []
    for degree in range(degree_channel_mixer.shape[0]):
        first_comp = degree * degree
        last_comp = (degree + 1) * (degree + 1)
        product_part = jnp.einsum(
            "ncd,de->nce",
            row_block[:, first_comp:last_comp, :],
            degree_channel_mixer[degree],
            preferred_element_type=jnp.float32,
        )
        pieces.append(product_part.astype(jnp.bfloat16))
    joined = jnp.concatenate(pieces, axis=1)
    return joined.reshape(row_block.shape[0], -1)


def readout_sum(message, affinity_output_head):
    result_sum = jnp.sum(message[:, 0, :] * affinity_output_head[0], axis=1)
    for degree in range(1, affinity_output_head.shape[0]):
        first_comp = degree * degree
        last_comp = (degree + 1) * (degree + 1)
        part_sq = message[:, first_comp:last_comp, :] * message[:, first_comp:last_comp, :]
        channel_norm = jnp.sqrt(jnp.sum(part_sq, axis=1) + 1e-06)
        result_sum = result_sum + jnp.sum(channel_norm * affinity_output_head[degree], axis=1)
    return result_sum


def shards(
    equivariant_embedding,
    cartesian_coordinates,
    element_identity,
    occupied_site_totals,
    halo_export_indices,
    adjacency_rows,
    attention_source_weights,
    attention_target_weights,
    degree_channel_mixer,
    affinity_output_head,
    baseline_affinity_per_element,
    chemical_stiffness,
    reciprocal_lattice_points,
    ewald_weighting,
):
    atom_slots = equivariant_embedding.shape[2]
    channels = equivariant_embedding.shape[4]
    own_feats = equivariant_embedding[0, 0]
    scalar_ch = own_feats[:, 0, :]
    queries = jnp.dot(
        scalar_ch, attention_source_weights, preferred_element_type=jnp.float32
    ).astype(jnp.bfloat16)
    own_keys = jnp.dot(
        scalar_ch, attention_target_weights, preferred_element_type=jnp.float32
    ).astype(jnp.bfloat16)
    own_values = project_values(own_feats, degree_channel_mixer)
    packed = jnp.concatenate([own_keys, own_values], axis=1)
    outgoing = packed[halo_export_indices[0, 0]]
    arrived = extended(outgoing[None, None], (("dom", 0), ("slab", 1)), 1)
    arrived = arrived.reshape(-1, packed.shape[1])
    table_keys = jnp.concatenate([own_keys, arrived[:, :channels]], axis=0)
    table_values = jnp.concatenate([own_values, arrived[:, channels:]], axis=0)
    table_size = table_keys.shape[0]
    neigh_dev = adjacency_rows[0, 0]
    columns = jnp.arange(table_size, dtype=jnp.int32)
    neighbour_mask = jnp.any(neigh_dev[:, :, None] == columns[None, None, :], axis=1)
    scores = jnp.einsum("ac,tc->at", queries, table_keys, preferred_element_type=jnp.float32)
    weights = jnp.where(
        neighbour_mask, jax.nn.sigmoid(scores / math.sqrt(channels)) * 0.125, 0.0
    ).astype(jnp.bfloat16)
    message = jnp.dot(weights, table_values, preferred_element_type=jnp.float32).reshape(
        atom_slots, -1, channels
    )
    element_hit = (
        element_identity[0, 0][:, None]
        == jnp.arange(baseline_affinity_per_element.shape[0], dtype=jnp.int32)[None, :]
    ).astype(jnp.float32)
    electroneg = readout_sum(message, affinity_output_head) + jnp.sum(
        element_hit * baseline_affinity_per_element[None, :], axis=1
    )
    chips_x = CHIPS_X
    chips_z = lax.axis_size("dom") // chips_x
    chips_y = lax.axis_size("slab") // 2
    charges, forces = equilibrate(
        (chips_x, chips_y, chips_z),
        (-electroneg).reshape(1, atom_slots),
        element_identity[0],
        occupied_site_totals,
        cartesian_coordinates[0, 0].reshape(3, 1, atom_slots),
        chemical_stiffness,
        reciprocal_lattice_points,
        ewald_weighting,
    )
    return (charges.reshape(1, 1, atom_slots), forces.reshape(1, 1, 3, atom_slots))


def solution(mesh):
    placed = (
        P("dom", "slab", None, None, None),
        P("dom", "slab", None, None),
        P("dom", "slab", None),
        P("dom", "slab"),
        P("dom", "slab", None),
        P("dom", "slab", None, None),
        P(),
        P(),
        P(),
        P(),
        P(),
        P(),
        P(),
        P(),
    )
    return jax.shard_map(
        shards,
        mesh=mesh,
        in_specs=placed,
        out_specs=(P("dom", "slab", None), P("dom", "slab", None, None)),
        check_vma=False,
    )
```

```python
import math

import jax
import jax.numpy as jnp
from jax import lax
from jax.experimental import pallas as pl
from jax.experimental.pallas import tpu as pltpu
from jax.sharding import PartitionSpec as P

ITERS = 4
CHIPS_X = 4
LANES = 128
MESH = pl.DeviceIdType.MESH
F32 = jnp.float32

HALF_PI_PARTS = (1.5703125, 4.837512969970703125e-4, 7.54978995489188216e-8)


def sine_cosine(phase):
    quadrant = jnp.round(phase * (2.0 / math.pi))
    reduced = phase - quadrant * HALF_PI_PARTS[0]
    reduced = reduced - quadrant * HALF_PI_PARTS[1]
    reduced = reduced - quadrant * HALF_PI_PARTS[2]
    square = reduced * reduced
    odd = (-1.9515295891e-4 * square + 8.3321608736e-3) * square - 1.6666654611e-1
    odd = odd * square * reduced + reduced
    even = (2.443315711809948e-5 * square - 1.388731625493765e-3) * square
    even = (even + 4.166664568298827e-2) * square * square - 0.5 * square + 1.0
    turn = quadrant.astype(jnp.int32)
    swap = (turn & 1) == 1
    sine = jnp.where(swap, even, odd)
    cosine = jnp.where(swap, odd, even)
    sine = jnp.where((turn & 2) == 2, -sine, sine)
    cosine = jnp.where(((turn + 1) & 2) == 2, -cosine, cosine)
    return sine, cosine


CHUNKS = 2
SCALARS = 3


def place_of(shape):
    chips_x, chips_y, chips_z = shape
    dom, slab = lax.axis_index("dom"), lax.axis_index("slab")
    return dom // chips_z, slab // 2, dom % chips_z, slab % 2


def device(shape, x, y, z, core):
    return (x * shape[2] + z, y * 2 + core)


def far_first(count):
    return sorted(range(1, count), key=lambda j: -min(j, count - j))


def sum_partners(shape):
    x, y, z, core = place_of(shape)
    chips_x, ring, _ = shape
    group = 2 * chips_x
    mine = x * 2 + core
    peers = []
    for i in far_first(group):
        other = (mine + i) % group
        peers.append((other, device(shape, other // 2, y, z, other % 2)))
    along = [
        device(shape, x, (y + j * (1 - core)) % ring, (z + j * core) % ring, core)
        for j in far_first(ring)
    ]
    across = [
        device(shape, x, (y + j * core) % ring, (z + j * (1 - core)) % ring, core)
        for j in far_first(ring)
    ]
    return mine, peers, along, across


def halo_partners(shape):
    x, y, z, core = place_of(shape)
    domains = shape[0] * shape[2]
    dom, slab = lax.axis_index("dom"), lax.axis_index("slab")
    way = 1 - 2 * core
    return {
        "before": ((dom + domains - 1) % domains, slab),
        "after": ((dom + 1) % domains, slab),
        "pair": (dom, y * 2 + 1 - core),
        "outer": (dom, (slab + 2 * shape[1] - way) % (2 * shape[1])),
        "ahead": ((dom + domains + way) % domains, slab),
    }


def row_of(column, eye):
    return jnp.sum(jnp.where(eye, column, 0.0), axis=0, keepdims=True)


def column_of(row, eye):
    wide = jnp.broadcast_to(row, (LANES, LANES))
    return jnp.broadcast_to(
        jnp.sum(jnp.where(eye, wide, 0.0), axis=1, keepdims=True), (LANES, LANES)
    )


def identity_mask(count):
    shape = (count, count)
    return lax.broadcasted_iota(jnp.int32, shape, 0) == lax.broadcasted_iota(jnp.int32, shape, 1)


def degrees_of(comps):
    return [range(l * l, (l + 1) * (l + 1)) for l in range(math.isqrt(comps))]


def fill_tables(first, stop, waves_ref, sites, cos_ref, sin_ref):
    step_rows = 32

    def per_block(block, carry):
        lanes = pl.ds(pl.multiple_of(block * LANES, LANES), LANES)

        def per_rows(part, inner):
            rows = pl.ds(pl.multiple_of(part * step_rows, step_rows), step_rows)
            phase = (
                sites[0, rows, :] * waves_ref[0:1, lanes]
                + sites[1, rows, :] * waves_ref[1:2, lanes]
                + sites[2, rows, :] * waves_ref[2:3, lanes]
            )
            sine, cosine = sine_cosine(phase)
            cos_ref[block, rows, :] = cosine
            sin_ref[block, rows, :] = sine
            return inner

        return lax.fori_loop(0, LANES // step_rows, per_rows, carry)

    lax.fori_loop(first, stop, per_block, 0)


def fill_mask(adjacency_ref, upright, mask_ref):
    size = upright.shape[0]
    ghosts = (size - LANES) // 8
    group = 64

    def per_group(part, carry):
        start = part * group
        row = lax.broadcasted_iota(jnp.int32, (group, LANES), 0) + start
        row = row + jnp.where(row >= LANES + 4 * ghosts, ghosts, 0)
        hit = row == adjacency_ref[0:1, :]
        for j in range(1, adjacency_ref.shape[0]):
            hit = hit | (row == adjacency_ref[j : j + 1, :])
        upright[pl.ds(pl.multiple_of(start, group), group), :] = jnp.where(hit, 1.0, 0.0)
        return carry

    lax.fori_loop(0, size // group, per_group, 0)
    for part in range(size // LANES):
        span = slice(part * LANES, (part + 1) * LANES)
        mask_ref[:, span] = upright[span, :].T


def attention(queries, keys, mask):
    scores = lax.dot_general(
        queries, keys, (((1,), (1,)), ((), ())), preferred_element_type=F32
    )
    gate = jax.nn.sigmoid(scores / math.sqrt(LANES)) * 0.125
    return jnp.where(mask > 0.0, gate, 0.0).astype(jnp.bfloat16)


def whole_kernel(
    shape,
    features_ref,
    place_ref,
    species_ref,
    count_ref,
    export_ref,
    adjacency_ref,
    source_ref,
    target_ref,
    mixer_ref,
    head_ref,
    baseline_ref,
    stiffness_ref,
    waves_ref,
    weight_ref,
    charges_ref,
    forces_ref,
    queries,
    table,
    outgoing,
    arrived,
    upright,
    mask_ref,
    own_message,
    cos_ref,
    sin_ref,
    sites,
    vectors,
    mine,
    parts,
    inbox,
    whole,
    total,
    weighted,
    halo_send,
    halo_recv,
    send_sem,
    recv_sem,
):
    group_index, peers, along, across = sum_partners(shape)
    near = halo_partners(shape)
    core = place_of(shape)[3]
    group = len(peers) + 1
    everyone = [peer for _, peer in peers] + along + across
    everyone += [near[name] for name in ("before", "after", "pair", "outer")]
    barrier = pltpu.get_barrier_semaphore()
    for partner in everyone:
        pl.semaphore_signal(barrier, inc=1, device_id=partner, device_id_type=MESH)

    comps = features_ref.shape[0]
    ghosts = outgoing.shape[1]
    blocks = cos_ref.shape[0]
    scale = 1.0 / math.sqrt(lax.axis_size("dom") * lax.axis_size("slab") * LANES)
    bf16 = jnp.bfloat16

    for degree, span in enumerate(degrees_of(comps)):
        for comp in span:
            product = jnp.dot(
                features_ref[comp], mixer_ref[degree], preferred_element_type=F32
            )
            table[comp] = product.astype(bf16)
    scalar = features_ref[0]
    table[comps] = jnp.dot(scalar, target_ref[...], preferred_element_type=F32).astype(bf16)
    queries[...] = jnp.dot(scalar, source_ref[...], preferred_element_type=F32).astype(bf16)
    offered = jnp.broadcast_to(export_ref[...], (ghosts, ghosts)).astype(F32)
    offered = jnp.sum(jnp.where(identity_mask(ghosts), offered, 0.0), axis=1, keepdims=True)
    slots = lax.broadcasted_iota(jnp.int32, (ghosts, LANES), 1).astype(F32)
    pick = jnp.where(slots == offered, 1.0, 0.0).astype(bf16)
    for comp in range(comps + 1):
        row = jnp.dot(pick, table[comp], preferred_element_type=F32)
        outgoing[comp] = row.astype(bf16)

    eye = identity_mask(LANES)
    for axis in range(3):
        sites[axis] = column_of(place_ref[axis], eye)
    species = species_ref[...]
    hardness = jnp.zeros(species.shape, F32)
    baseline = jnp.zeros(species.shape, F32)
    for element in range(stiffness_ref.shape[0]):
        hardness = jnp.where(species == element, stiffness_ref[element], hardness)
        baseline = jnp.where(species == element, baseline_ref[element], baseline)
    live = lax.broadcasted_iota(jnp.int32, (1, LANES), 1) < count_ref[0, 0]
    vectors[0] = column_of(baseline, eye)
    vectors[1] = jnp.zeros((LANES, LANES), F32)
    vectors[2] = jnp.zeros((LANES, LANES), F32)
    vectors[3] = column_of(hardness, eye)
    vectors[4] = column_of(jnp.where(live, 1.0, 0.0), eye)
    total[...] = jnp.zeros_like(total)

    pl.semaphore_wait(barrier, len(everyone))

    size = (comps + 1) // CHUNKS

    def ship(number, chunk, source, slot, target):
        span = pl.ds(chunk * size, size)
        return pltpu.make_async_remote_copy(
            src_ref=source,
            dst_ref=arrived.at[span, slot],
            send_sem=halo_send.at[number * CHUNKS + chunk],
            recv_sem=halo_recv.at[number * CHUNKS + chunk],
            device_id=target,
            device_id_type=MESH,
        )

    def own(chunk):
        return outgoing.at[pl.ds(chunk * size, size)]

    def got(chunk, slot):
        return arrived.at[pl.ds(chunk * size, size), slot]

    sent = {}
    for chunk in range(CHUNKS):
        sent["after", chunk] = ship(0, chunk, own(chunk), 1, near["after"])
        sent["before", chunk] = ship(1, chunk, own(chunk), 6, near["before"])
        sent["outer", chunk] = ship(2, chunk, own(chunk), 4 - core, near["outer"])
        sent["pair", chunk] = ship(3, chunk, own(chunk), 3 + core, near["pair"])
        for name in ("after", "before", "outer", "pair"):
            sent[name, chunk].start()

    fill_mask(adjacency_ref, upright, mask_ref)
    own_weights = attention(queries[...], table[comps], mask_ref[:, 0:LANES])
    for comp in range(comps):
        own_message[comp] = jnp.dot(own_weights, table[comp], preferred_element_type=F32)

    for chunk in range(CHUNKS):
        fill_tables(
            chunk * blocks // CHUNKS, (chunk + 1) * blocks // CHUNKS, waves_ref, sites, cos_ref, sin_ref
        )
        sent["outer", chunk].wait_recv()
        sent["ring", chunk] = ship(4, chunk, got(chunk, 3 + core), 7 * core, near["ahead"])
        sent["ring", chunk].start()
        sent["after", chunk].wait_recv()
        sent["before", chunk].wait_recv()
        sent["cross", chunk] = ship(5, chunk, got(chunk, 1 + 5 * core), 2 + 3 * core, near["outer"])
        sent["low", chunk] = ship(6, chunk, got(chunk, 1), 2 * core, near["pair"])
        sent["high", chunk] = ship(7, chunk, got(chunk, 6), 5 + 2 * core, near["pair"])
        for name in ("cross", "low", "high"):
            sent[name, chunk].start()
    for chunk in range(CHUNKS):
        for name in ("pair", "ring", "cross", "low", "high"):
            sent[name, chunk].wait_recv()

    ghost_keys = arrived[comps].reshape(8 * ghosts, LANES)
    weights = attention(queries[...], ghost_keys, mask_ref[:, LANES:])
    readout = jnp.zeros((LANES, LANES), F32)
    for degree, span in enumerate(degrees_of(comps)):
        square = jnp.zeros((LANES, LANES), F32)
        for comp in span:
            message = own_message[comp] + jnp.dot(
                weights, arrived[comp].reshape(8 * ghosts, LANES), preferred_element_type=F32
            )
            square = message if degree == 0 else square + message * message
        norm = square if degree == 0 else jnp.sqrt(square + 1e-06)
        readout = readout + norm * head_ref[degree : degree + 1, :]
    electroneg = jnp.sum(readout, axis=1, keepdims=True) + vectors[0]
    vectors[0] = vectors[4] * -electroneg
    for item in sent.values():
        item.wait_send()

    piece = mine.shape[1] - SCALARS
    halves = group // 2

    def copy(turn, number, source, drop, target):
        return pltpu.make_async_remote_copy(
            src_ref=source,
            dst_ref=drop,
            send_sem=send_sem.at[number],
            recv_sem=recv_sem.at[turn, number],
            device_id=target,
            device_id_type=MESH,
        )

    def global_sum(turn):
        started = []
        for other, target in peers:
            number = len(started)
            started.append(copy(turn, number, mine.at[other], inbox.at[turn, number], target))
            started[-1].start()
        held = mine[group_index]
        for number in range(len(peers)):
            started[number].wait_recv()
            held = held + inbox[turn, number]
        for stage, targets in enumerate((along, across)):
            parts[stage] = held
            first = len(started)
            for target in targets:
                number = len(started)
                started.append(copy(turn, number, parts.at[stage], inbox.at[turn, number], target))
                started[-1].start()
            for number in range(first, len(started)):
                started[number].wait_recv()
                held = held + inbox[turn, number]
        parts[2] = held
        first = len(started)
        for _, target in peers:
            number = len(started)
            drop = whole.at[turn, group_index]
            started.append(copy(turn, number, parts.at[2], drop, target))
            started[-1].start()
        whole[turn, group_index] = held
        for item in started[first:]:
            item.wait_recv()
        for item in started:
            item.wait_send()

    def iteration(turn, carry):
        previous_norm, stiff_part = carry
        residual, hard = vectors[0], vectors[3]
        hard_residual = hard * residual

        def project(part, inner):
            for j in range(piece):
                block = part * piece + j
                mine[part, j : j + 1, :] = jnp.sum(
                    cos_ref[block] * residual, axis=0, keepdims=True
                )
                mine[part + halves, j : j + 1, :] = jnp.sum(
                    sin_ref[block] * residual, axis=0, keepdims=True
                )
            return inner

        lax.fori_loop(0, halves, project, 0)
        scalars = (residual * residual, hard_residual * residual, hard_residual * vectors[1])
        for i, product in enumerate(scalars):
            row = jnp.sum(product, axis=0, keepdims=True)
            for part in range(group):
                mine[part, piece + i : piece + i + 1, :] = row
        global_sum(turn)
        norm, pure, mixed = (
            whole[turn, 0, piece + i : piece + i + 1, :] for i in range(SCALARS)
        )
        beta = jnp.where(turn > 0, norm / previous_norm, 0.0)
        stiff_part = pure + 2.0 * beta * mixed + beta * beta * stiff_part
        weight = weight_ref[...]
        recip = jnp.zeros_like(weight)
        for part in range(2):
            factors = whole[turn, pl.ds(part * halves, halves), 0:piece, :]
            factors = factors.reshape(blocks, LANES) + beta * total[part]
            total[part] = factors
            weighted[part] = weight * factors
            recip = recip + weight * factors * factors
        recip = jnp.sum(jnp.sum(recip, axis=0, keepdims=True), axis=1, keepdims=True)
        step = norm / (stiff_part + scale * recip)
        direction = residual + beta * vectors[1]
        vectors[1] = direction

        def back(part, acc):
            for j in range(2):
                block = part * 2 + j
                row = pl.ds(block, 1)
                acc = acc + cos_ref[block] * weighted[0, row, :]
                acc = acc + sin_ref[block] * weighted[1, row, :]
            return acc

        image = lax.fori_loop(0, blocks // 2, back, jnp.zeros((LANES, LANES), F32))
        image = hard * direction + scale * jnp.sum(image, axis=1, keepdims=True)
        image = vectors[4] * image
        vectors[2] = vectors[2] + step * direction
        vectors[0] = residual - step * image
        for part in range(2):
            total[2 + part] = total[2 + part] + step * weighted[part]
        return norm, stiff_part

    ones = jnp.ones((1, LANES), F32)
    lax.fori_loop(0, ITERS, iteration, (ones, ones))

    charges = vectors[2]
    charges_ref[...] = row_of(charges, eye)
    half = LANES // 2
    for part in range(2):
        rows = pl.ds(part * half, half)

        def field(block, acc):
            row = pl.ds(block, 1)
            lanes = pl.ds(pl.multiple_of(block * LANES, LANES), LANES)
            term = (
                sin_ref[block, rows, :] * total[2, row, :]
                - cos_ref[block, rows, :] * total[3, row, :]
            )
            return tuple(acc[axis] + term * waves_ref[axis : axis + 1, lanes] for axis in range(3))

        zero = jnp.zeros((half, LANES), F32)
        field_parts = lax.fori_loop(0, blocks, field, (zero, zero, zero))
        for axis in range(3):
            column = scale * jnp.sum(field_parts[axis], axis=1, keepdims=True)
            sites[axis, rows, :] = jnp.broadcast_to(column, (half, LANES))
    for axis in range(3):
        forces_ref[axis] = row_of(charges * sites[axis], eye)


def shards(
    equivariant_embedding,
    cartesian_coordinates,
    element_identity,
    occupied_site_totals,
    halo_export_indices,
    adjacency_rows,
    attention_source_weights,
    attention_target_weights,
    degree_channel_mixer,
    affinity_output_head,
    baseline_affinity_per_element,
    chemical_stiffness,
    reciprocal_lattice_points,
    ewald_weighting,
):
    chips_x = CHIPS_X
    ring = lax.axis_size("slab") // 2
    shape = (chips_x, ring, lax.axis_size("dom") // chips_x)
    assert shape[1] == shape[2]
    comps = equivariant_embedding.shape[3]
    ghosts = halo_export_indices.shape[2]
    blocks = reciprocal_lattice_points.shape[1] // LANES
    group = 2 * chips_x
    rows = 2 * blocks // group + SCALARS
    copies = 2 * (group - 1) + 2 * (ring - 1)
    table_size = LANES + 8 * ghosts
    bf16 = jnp.bfloat16
    vmem = pl.BlockSpec(memory_space=pltpu.VMEM)
    smem = pl.BlockSpec(memory_space=pltpu.SMEM)
    charges, forces = pl.pallas_call(
        lambda *refs: whole_kernel(shape, *refs),
        name="equilibrate",
        out_shape=(
            jax.ShapeDtypeStruct((1, LANES), F32),
            jax.ShapeDtypeStruct((3, 1, LANES), F32),
        ),
        in_specs=[vmem, vmem, vmem, smem, vmem, vmem, vmem, vmem, vmem, vmem, smem, smem, vmem, vmem],
        out_specs=(vmem, vmem),
        scratch_shapes=[
            pltpu.VMEM((LANES, LANES), bf16),
            pltpu.VMEM((comps + 1, LANES, LANES), bf16),
            pltpu.VMEM((comps + 1, ghosts, LANES), bf16),
            pltpu.VMEM((comps + 1, 8, ghosts, LANES), bf16),
            pltpu.VMEM((table_size, LANES), F32),
            pltpu.VMEM((LANES, table_size), F32),
            pltpu.VMEM((comps, LANES, LANES), F32),
            pltpu.VMEM((blocks, LANES, LANES), F32),
            pltpu.VMEM((blocks, LANES, LANES), F32),
            pltpu.VMEM((3, LANES, LANES), F32),
            pltpu.VMEM((5, LANES, LANES), F32),
            pltpu.VMEM((group, rows, LANES), F32),
            pltpu.VMEM((3, rows, LANES), F32),
            pltpu.VMEM((ITERS, copies - group + 1, rows, LANES), F32),
            pltpu.VMEM((ITERS, group, rows, LANES), F32),
            pltpu.VMEM((4, blocks, LANES), F32),
            pltpu.VMEM((2, blocks, LANES), F32),
            pltpu.SemaphoreType.DMA((8 * CHUNKS,)),
            pltpu.SemaphoreType.DMA((8 * CHUNKS,)),
            pltpu.SemaphoreType.DMA((copies,)),
            pltpu.SemaphoreType.DMA((ITERS, copies)),
        ],
        compiler_params=pltpu.CompilerParams(
            collective_id=1, has_side_effects=True, vmem_limit_bytes=48 * 1024 * 1024
        ),
    )(
        jnp.transpose(equivariant_embedding[0, 0], (1, 0, 2)),
        cartesian_coordinates[0, 0].reshape(3, 1, LANES),
        element_identity[0],
        occupied_site_totals,
        halo_export_indices[0],
        adjacency_rows[0, 0].T,
        attention_source_weights,
        attention_target_weights,
        degree_channel_mixer,
        affinity_output_head,
        baseline_affinity_per_element,
        chemical_stiffness,
        reciprocal_lattice_points,
        ewald_weighting.reshape(blocks, LANES),
    )
    return (charges.reshape(1, 1, LANES), forces.reshape(1, 1, 3, LANES))


def solution(mesh):
    placed = (
        P("dom", "slab", None, None, None),
        P("dom", "slab", None, None),
        P("dom", "slab", None),
        P("dom", "slab"),
        P("dom", "slab", None),
        P("dom", "slab", None, None),
        P(),
        P(),
        P(),
        P(),
        P(),
        P(),
        P(),
        P(),
    )
    return jax.shard_map(
        shards,
        mesh=mesh,
        in_specs=placed,
        out_specs=(P("dom", "slab", None), P("dom", "slab", None, None)),
        check_vma=False,
    )
```

```python
import math

import jax
import jax.numpy as jnp
from jax import lax
from jax.experimental import pallas as pl
from jax.experimental.pallas import tpu as pltpu
from jax.sharding import PartitionSpec as P

ITERS = 4
CHIPS_X = 4
LANES = 128
MESH = pl.DeviceIdType.MESH
F32 = jnp.float32

HALF_PI_PARTS = (1.5703125, 4.837512969970703125e-4, 7.54978995489188216e-8)


def sine_cosine(phase):
    quadrant = jnp.round(phase * (2.0 / math.pi))
    reduced = phase - quadrant * HALF_PI_PARTS[0]
    reduced = reduced - quadrant * HALF_PI_PARTS[1]
    reduced = reduced - quadrant * HALF_PI_PARTS[2]
    square = reduced * reduced
    odd = (-1.9515295891e-4 * square + 8.3321608736e-3) * square - 1.6666654611e-1
    odd = odd * square * reduced + reduced
    even = (2.443315711809948e-5 * square - 1.388731625493765e-3) * square
    even = (even + 4.166664568298827e-2) * square * square - 0.5 * square + 1.0
    turn = quadrant.astype(jnp.int32)
    swap = (turn & 1) == 1
    sine = jnp.where(swap, even, odd)
    cosine = jnp.where(swap, odd, even)
    sine = jnp.where((turn & 2) == 2, -sine, sine)
    cosine = jnp.where(((turn + 1) & 2) == 2, -cosine, cosine)
    return sine, cosine


CHUNKS = 2
SCALARS = 3
TILE = 8


def place_of(shape):
    chips_x, chips_y, chips_z = shape
    dom, slab = lax.axis_index("dom"), lax.axis_index("slab")
    return dom // chips_z, slab // 2, dom % chips_z, slab % 2


def device(shape, x, y, z, core):
    return (x * shape[2] + z, y * 2 + core)


def far_first(count):
    return sorted(range(1, count), key=lambda j: -min(j, count - j))


def sum_partners(shape):
    x, y, z, core = place_of(shape)
    chips_x, ring, _ = shape
    group = 2 * chips_x
    mine = x * 2 + core
    peers = []
    for i in far_first(group):
        other = (mine + i) % group
        peers.append((other, device(shape, other // 2, y, z, other % 2)))
    along = [
        device(shape, x, (y + j * (1 - core)) % ring, (z + j * core) % ring, core)
        for j in far_first(ring)
    ]
    across = [
        device(shape, x, (y + j * core) % ring, (z + j * (1 - core)) % ring, core)
        for j in far_first(ring)
    ]
    return mine, peers, along, across


def halo_partners(shape):
    x, y, z, core = place_of(shape)
    domains = shape[0] * shape[2]
    dom, slab = lax.axis_index("dom"), lax.axis_index("slab")
    way = 1 - 2 * core
    return {
        "before": ((dom + domains - 1) % domains, slab),
        "after": ((dom + 1) % domains, slab),
        "pair": (dom, y * 2 + 1 - core),
        "outer": (dom, (slab + 2 * shape[1] - way) % (2 * shape[1])),
        "ahead": ((dom + domains + way) % domains, slab),
    }


def row_of(column, eye):
    return jnp.sum(jnp.where(eye, column, 0.0), axis=0, keepdims=True)


def identity_mask(count):
    shape = (count, count)
    return lax.broadcasted_iota(jnp.int32, shape, 0) == lax.broadcasted_iota(jnp.int32, shape, 1)


def degrees_of(comps):
    return [range(l * l, (l + 1) * (l + 1)) for l in range(math.isqrt(comps))]


def fill_mask(adjacency_ref, upright, mask_ref):
    size = upright.shape[0]
    ghosts = (size - LANES) // 8
    group = 64

    def per_group(part, carry):
        start = part * group
        row = lax.broadcasted_iota(jnp.int32, (group, LANES), 0) + start
        row = row + jnp.where(row >= LANES + 4 * ghosts, ghosts, 0)
        hit = row == adjacency_ref[0:1, :]
        for j in range(1, adjacency_ref.shape[0]):
            hit = hit | (row == adjacency_ref[j : j + 1, :])
        upright[pl.ds(pl.multiple_of(start, group), group), :] = jnp.where(hit, 1.0, 0.0)
        return carry

    lax.fori_loop(0, size // group, per_group, 0)
    for part in range(size // LANES):
        span = slice(part * LANES, (part + 1) * LANES)
        mask_ref[:, span] = upright[span, :].T


def attention(queries, keys, mask):
    scores = lax.dot_general(
        queries, keys, (((1,), (1,)), ((), ())), preferred_element_type=F32
    )
    gate = jax.nn.sigmoid(scores / math.sqrt(LANES)) * 0.125
    return jnp.where(mask > 0.0, gate, 0.0).astype(jnp.bfloat16)


def spread(rows):
    return jnp.concatenate([rows] * (LANES // rows.shape[0]), axis=0).T


def wide(columns, index):
    return jnp.broadcast_to(columns[:, index : index + 1], (LANES, LANES))


def fill_tables(first, stop, blocks, waves, about, sites, cos_ref, sin_ref):
    step_rows = 64

    def per_member(member, carry):
        columns = spread(about[member])
        for axis in range(3):
            sites[axis] = wide(columns, axis)

        def per_rows(part, inner):
            block, rows = part // (LANES // step_rows), part % (LANES // step_rows)
            lanes = pl.ds(pl.multiple_of(block * LANES, LANES), LANES)
            rows = pl.ds(pl.multiple_of(rows * step_rows, step_rows), step_rows)
            phase = (
                sites[0, rows, :] * waves[0:1, lanes]
                + sites[1, rows, :] * waves[1:2, lanes]
                + sites[2, rows, :] * waves[2:3, lanes]
            )
            sine, cosine = sine_cosine(phase)
            cos_ref[member * blocks + block, rows, :] = cosine
            sin_ref[member * blocks + block, rows, :] = sine
            return inner

        return lax.fori_loop(0, blocks * LANES // step_rows, per_rows, carry)

    lax.fori_loop(first, stop, per_member, 0)


def whole_kernel(
    shape,
    features_hbm,
    mixer_hbm,
    source_hbm,
    target_hbm,
    export_hbm,
    place_hbm,
    species_hbm,
    adjacency_hbm,
    head_hbm,
    weight_hbm,
    waves_hbm,
    count_ref,
    baseline_ref,
    stiffness_ref,
    charges_ref,
    forces_ref,
    features_ref,
    mixer_ref,
    source_ref,
    target_ref,
    export_ref,
    place_ref,
    species_ref,
    adjacency_ref,
    head_ref,
    weight_ref,
    waves,
    queries,
    table,
    outgoing,
    arrived,
    upright,
    mask_ref,
    own_message,
    cos_ref,
    sin_ref,
    sites,
    about,
    first_rows,
    vectors,
    parts,
    inbox,
    ring_total,
    factors,
    posts,
    post_inbox,
    post_total,
    matrix,
    fields,
    field_inbox,
    load_sem,
    halo_send,
    halo_recv,
    near_recv,
    group_send,
    group_recv,
    ring_send,
    ring_recv,
):
    me, peers, along, across = sum_partners(shape)
    near = halo_partners(shape)
    core = place_of(shape)[3]
    group = len(peers) + 1
    everyone = [peer for _, peer in peers] + along + across
    everyone += [near[name] for name in ("before", "after", "pair", "outer")]
    barrier = pltpu.get_barrier_semaphore()
    for partner in everyone:
        pl.semaphore_signal(barrier, inc=1, device_id=partner, device_id_type=MESH)

    comps = features_ref.shape[0]
    ghosts = outgoing.shape[1]
    blocks = cos_ref.shape[0] // group
    span = blocks * LANES
    scale = 1.0 / math.sqrt(lax.axis_size("dom") * lax.axis_size("slab") * LANES)
    bf16 = jnp.bfloat16

    own_waves = waves_hbm.at[:, pl.ds(pl.multiple_of(me * span, LANES), span)]
    loads = [
        pltpu.make_async_copy(source, target, load_sem.at[i])
        for i, (source, target) in enumerate(
            (
                (features_hbm, features_ref),
                (mixer_hbm, mixer_ref),
                (source_hbm, source_ref),
                (target_hbm, target_ref),
                (export_hbm, export_ref),
                (place_hbm, place_ref),
                (species_hbm, species_ref),
                (adjacency_hbm, adjacency_ref),
                (head_hbm, head_ref),
                (weight_hbm, weight_ref),
                (own_waves, waves),
            )
        )
    ]
    for item in loads:
        item.start()
    eye = identity_mask(LANES)

    loads[5].wait()
    loads[6].wait()
    species = species_ref[...]
    hardness = jnp.zeros(species.shape, F32)
    baseline = jnp.zeros(species.shape, F32)
    for element in range(stiffness_ref.shape[0]):
        hardness = jnp.where(species == element, stiffness_ref[element], hardness)
        baseline = jnp.where(species == element, baseline_ref[element], baseline)
    live = lax.broadcasted_iota(jnp.int32, (1, LANES), 1) < count_ref[0, 0]
    live = jnp.where(live, 1.0, 0.0)
    about[me] = jnp.zeros((TILE, LANES), F32)
    for axis in range(3):
        about[me, axis : axis + 1, :] = place_ref[axis]
    about[me, 3:4, :] = hardness
    about[me, 4:5, :] = live

    for i in range(5):
        loads[i].wait()
    for degree, members in enumerate(degrees_of(comps)):
        for comp in members:
            product = jnp.dot(
                features_ref[comp], mixer_ref[degree], preferred_element_type=F32
            )
            table[comp] = product.astype(bf16)
    scalar = features_ref[0]
    table[comps] = jnp.dot(scalar, target_ref[...], preferred_element_type=F32).astype(bf16)
    queries[...] = jnp.dot(scalar, source_ref[...], preferred_element_type=F32).astype(bf16)
    offered = jnp.broadcast_to(export_ref[...], (ghosts, ghosts)).astype(F32)
    offered = jnp.sum(jnp.where(identity_mask(ghosts), offered, 0.0), axis=1, keepdims=True)
    slots = lax.broadcasted_iota(jnp.int32, (ghosts, LANES), 1).astype(F32)
    pick = jnp.where(slots == offered, 1.0, 0.0).astype(bf16)
    for comp in range(comps + 1):
        row = jnp.dot(pick, table[comp], preferred_element_type=F32)
        outgoing[comp] = row.astype(bf16)

    pl.semaphore_wait(barrier, len(everyone))

    size = (comps + 1) // CHUNKS

    def ship(chunk, source, slot, target, sem):
        rows = pl.ds(chunk * size, size)
        copy = pltpu.make_async_remote_copy(
            src_ref=source,
            dst_ref=arrived.at[rows, slot],
            send_sem=halo_send,
            recv_sem=sem,
            device_id=target,
            device_id_type=MESH,
        )
        copy.start()

    def own(chunk):
        return outgoing.at[pl.ds(chunk * size, size)]

    def got(chunk, slot):
        return arrived.at[pl.ds(chunk * size, size), slot]

    def all_of(ref, send, receive):
        return pltpu.make_async_remote_copy(
            src_ref=ref,
            dst_ref=ref,
            send_sem=send,
            recv_sem=receive,
            device_id=near["pair"],
            device_id_type=MESH,
        )

    def to_group(pieces, drops, stage):
        for i, (_, target) in enumerate(peers):
            pltpu.make_async_remote_copy(
                src_ref=pieces(i),
                dst_ref=drops(i),
                send_sem=group_send.at[stage],
                recv_sem=group_recv.at[stage],
                device_id=target,
                device_id_type=MESH,
            ).start()

    for chunk in range(CHUNKS):
        ship(chunk, own(chunk), 1, near["after"], near_recv.at[chunk, 0])
        ship(chunk, own(chunk), 6, near["before"], near_recv.at[chunk, 0])
        ship(chunk, own(chunk), 4 - core, near["outer"], near_recv.at[chunk, 1])
        ship(chunk, own(chunk), 3 + core, near["pair"], halo_recv)
        if chunk == 0:
            to_group(lambda i: about.at[me], lambda i: about.at[me], 0)

    loads[7].wait()
    fill_mask(adjacency_ref, upright, mask_ref)
    own_weights = attention(queries[...], table[comps], mask_ref[:, 0:LANES])
    for comp in range(comps):
        own_message[comp] = jnp.dot(own_weights, table[comp], preferred_element_type=F32)

    for i in range(8, 11):
        loads[i].wait()
    others = about.at[pl.ds(0, group - 1)]
    all_of(others, group_send.at[0], group_recv.at[0]).wait_recv()
    for chunk in range(CHUNKS):
        fill_tables(
            chunk * group // CHUNKS,
            (chunk + 1) * group // CHUNKS,
            blocks,
            waves,
            about,
            sites,
            cos_ref,
            sin_ref,
        )
        all_of(got(chunk, 0), halo_send, near_recv.at[chunk, 1]).wait_recv()
        ship(chunk, got(chunk, 3 + core), 7 * core, near["ahead"], halo_recv)
        both = arrived.at[pl.ds(chunk * size, size), pl.ds(0, 2)]
        all_of(both, halo_send, near_recv.at[chunk, 0]).wait_recv()
        ship(chunk, got(chunk, 1 + 5 * core), 2 + 3 * core, near["outer"], halo_recv)
        ship(chunk, got(chunk, 1), 2 * core, near["pair"], halo_recv)
        ship(chunk, got(chunk, 6), 5 + 2 * core, near["pair"], halo_recv)
    for member in range(group):
        vectors[3, member : member + 1, :] = about[member, 3:4, :]
        vectors[4, member : member + 1, :] = about[member, 4:5, :]
    vectors[1] = jnp.zeros((group, LANES), F32)
    vectors[2] = jnp.zeros((group, LANES), F32)
    factors[...] = jnp.zeros_like(factors)
    all_of(arrived.at[:, pl.ds(0, 5)], halo_send, halo_recv).wait_recv()

    ghost_keys = arrived[comps].reshape(8 * ghosts, LANES)
    weights = attention(queries[...], ghost_keys, mask_ref[:, LANES:])
    readout = jnp.zeros((LANES, LANES), F32)
    for degree, members in enumerate(degrees_of(comps)):
        square = jnp.zeros((LANES, LANES), F32)
        for comp in members:
            message = own_message[comp] + jnp.dot(
                weights, arrived[comp].reshape(8 * ghosts, LANES), preferred_element_type=F32
            )
            square = message if degree == 0 else square + message * message
        norm = square if degree == 0 else jnp.sqrt(square + 1e-06)
        readout = readout + norm * head_ref[degree : degree + 1, :]
    electroneg = row_of(jnp.sum(readout, axis=1, keepdims=True), eye) + baseline
    first_rows[me] = -electroneg * live
    to_group(lambda i: first_rows.at[me], lambda i: first_rows.at[me], 1)
    all_of(arrived, halo_send, halo_recv).wait_send()
    all_of(others, group_send.at[0], group_recv.at[0]).wait_send()
    starts = first_rows.at[pl.ds(0, group - 1)]
    all_of(starts, group_send.at[1], group_recv.at[1]).wait()
    for member in range(group):
        vectors[0, member : member + 1, :] = first_rows[member]

    lanes = lax.broadcasted_iota(jnp.int32, (LANES, LANES), 1)
    scalar_row = 2 * blocks
    weight = weight_ref[me]
    tables = (cos_ref, sin_ref)

    def full_sum(rows):
        return jnp.sum(jnp.sum(rows, axis=0, keepdims=True), axis=1, keepdims=True)

    def project(turn):
        residual = vectors[0]
        columns = spread(residual)
        sums = [[jnp.zeros((TILE, LANES), F32) for _ in range(blocks)] for _ in range(2)]
        for member in range(group):
            column = wide(columns, member)
            for part in range(2):
                for block in range(blocks):
                    product = tables[part][member * blocks + block] * column
                    product = product.reshape(LANES // TILE, TILE, LANES)
                    sums[part][block] = sums[part][block] + jnp.sum(product, axis=0)
        for part in range(2):
            for block in range(blocks):
                row = part * blocks + block
                parts[turn, 0, row : row + 1, :] = jnp.sum(
                    sums[part][block], axis=0, keepdims=True
                )
        hard_residual = vectors[3] * residual
        scalars = (residual * residual, hard_residual * residual, hard_residual * vectors[1])
        for i, product in enumerate(scalars):
            row = scalar_row + i
            parts[turn, 0, row : row + 1, :] = jnp.broadcast_to(full_sum(product), (1, LANES))

    def ring_sum(turn, meanwhile):
        held = parts[turn, 0]
        for stage, targets in enumerate((along, across)):
            if stage > 0:
                parts[turn, stage] = held
            for i, target in enumerate(targets):
                pltpu.make_async_remote_copy(
                    src_ref=parts.at[turn, stage],
                    dst_ref=inbox.at[turn, stage, i],
                    send_sem=ring_send.at[stage],
                    recv_sem=ring_recv.at[turn, stage],
                    device_id=target,
                    device_id_type=MESH,
                ).start()
            if stage == 0:
                meanwhile()
            all_of(inbox.at[turn, stage], ring_send.at[stage], ring_recv.at[turn, stage]).wait()
            for i in range(len(targets)):
                held = held + inbox[turn, stage, i]
        ring_total[...] = held

    def follow(turn, previous_norm, stiff_part):
        norm, pure, mixed = (
            ring_total[scalar_row + i : scalar_row + i + 1, :] for i in range(SCALARS)
        )
        beta = jnp.where(turn > 0, norm / previous_norm, 0.0)
        stiff_part = pure + 2.0 * beta * mixed + beta * beta * stiff_part
        recip = jnp.zeros_like(weight)
        for part in range(2):
            rows = ring_total[part * blocks : (part + 1) * blocks, :] + beta * factors[part]
            factors[part] = rows
            factors[2 + part] = weight * rows
            recip = recip + weight * rows * rows
        vectors[1] = vectors[0] + beta * vectors[1]
        return norm, stiff_part, jnp.broadcast_to(full_sum(recip), (1, LANES))

    def iteration(turn, carry):
        project(turn)
        ring_sum(turn, lambda: None)
        norm, stiff_part, recip = follow(turn, *carry)

        def back(member, acc):
            image = jnp.zeros((LANES, LANES), F32)
            for block in range(blocks):
                for part in range(2):
                    row = factors[2 + part, block : block + 1, :]
                    image = image + tables[part][member * blocks + block] * row
            return jnp.where(lanes == member, jnp.sum(image, axis=1, keepdims=True), acc)

        images = lax.fori_loop(0, group, back, jnp.zeros((LANES, LANES), F32))
        posts[turn, 0:group, :] = images.T[0:group, :]
        posts[turn, group : group + 1, :] = recip
        to_group(lambda i: posts.at[turn], lambda i: post_inbox.at[turn, i], 2 + turn)
        held = posts[turn]
        all_of(post_inbox.at[turn], group_send.at[2 + turn], group_recv.at[2 + turn]).wait()
        for i in range(group - 1):
            held = held + post_inbox[turn, i]
        post_total[...] = held
        step = norm / (stiff_part + scale * post_total[group : group + 1, :])
        direction = vectors[1]
        image = vectors[4] * (vectors[3] * direction + scale * post_total[0:group, :])
        vectors[2] = vectors[2] + step * direction
        vectors[0] = vectors[0] - step * image
        for part in range(2):
            factors[4 + part] = factors[4 + part] + step * factors[2 + part]
        return norm, stiff_part

    def field_of(first, offset):
        half = LANES // 2

        def per_member(member, carry):
            for part in range(2):
                rows = pl.ds(part * half, half)
                sums = [jnp.zeros((half, LANES), F32) for _ in range(3)]
                for block in range(blocks):
                    where = member * blocks + block
                    term = (
                        sin_ref[where, rows, :] * factors[first, block : block + 1, :]
                        - cos_ref[where, rows, :] * factors[first + 1, block : block + 1, :]
                    )
                    for axis in range(3):
                        wave = waves[axis : axis + 1, block * LANES : (block + 1) * LANES]
                        sums[axis] = sums[axis] + term * wave
                filled = matrix[rows, :]
                for axis in range(3):
                    column = jnp.sum(sums[axis], axis=1, keepdims=True)
                    place = member * TILE + offset + axis
                    filled = jnp.where(lanes[0:half, :] == place, column, filled)
                matrix[rows, :] = filled
            return carry

        lax.fori_loop(0, group, per_member, 0)

    ones = jnp.ones((1, LANES), F32)
    carry = lax.fori_loop(0, ITERS - 1, iteration, (ones, ones))

    turn = ITERS - 1
    matrix[...] = jnp.zeros_like(matrix)
    project(turn)
    ring_sum(turn, lambda: field_of(4, 0))
    norm, stiff_part, recip = follow(turn, *carry)
    field_of(2, 3)
    field_rows = matrix[...].T
    for member in range(group):
        fields[member] = field_rows[member * TILE : (member + 1) * TILE, :]
        fields[member, 6:7, :] = recip
    stage = 1 + ITERS
    to_group(lambda i: fields.at[peers[i][0]], lambda i: field_inbox.at[i], stage)
    held = fields[me]
    all_of(field_inbox, group_send.at[stage], group_recv.at[stage]).wait()
    for i in range(group - 1):
        held = held + field_inbox[i]
    fields[me] = held
    step = norm / (stiff_part + scale * fields[me, 6:7, :])
    vectors[2] = vectors[2] + step * vectors[1]
    charges = vectors[2, pl.ds(me, 1), :]
    charges_ref[...] = charges
    for axis in range(3):
        field = fields[me, axis : axis + 1, :] + step * fields[me, 3 + axis : 4 + axis, :]
        forces_ref[axis] = charges * (scale * field)


def shards(
    equivariant_embedding,
    cartesian_coordinates,
    element_identity,
    occupied_site_totals,
    halo_export_indices,
    adjacency_rows,
    attention_source_weights,
    attention_target_weights,
    degree_channel_mixer,
    affinity_output_head,
    baseline_affinity_per_element,
    chemical_stiffness,
    reciprocal_lattice_points,
    ewald_weighting,
):
    chips_x = CHIPS_X
    ring = lax.axis_size("slab") // 2
    shape = (chips_x, ring, lax.axis_size("dom") // chips_x)
    assert shape[1] == shape[2]
    comps = equivariant_embedding.shape[3]
    ghosts = halo_export_indices.shape[2]
    degrees = degree_channel_mixer.shape[0]
    lists = adjacency_rows.shape[3]
    group = 2 * chips_x
    blocks = reciprocal_lattice_points.shape[1] // LANES // group
    rows = 2 * blocks + SCALARS
    table_size = LANES + 8 * ghosts
    bf16, i32 = jnp.bfloat16, jnp.int32
    assert group * TILE <= LANES and (comps + 1) % CHUNKS == 0
    vmem = pl.BlockSpec(memory_space=pltpu.VMEM)
    smem = pl.BlockSpec(memory_space=pltpu.SMEM)
    hbm = pl.BlockSpec(memory_space=pltpu.HBM)
    dma = pltpu.SemaphoreType.DMA
    charges, forces = pl.pallas_call(
        lambda *refs: whole_kernel(shape, *refs),
        name="equilibrate",
        out_shape=(
            jax.ShapeDtypeStruct((1, LANES), F32),
            jax.ShapeDtypeStruct((3, 1, LANES), F32),
        ),
        in_specs=[hbm] * 11 + [smem] * 3,
        out_specs=(vmem, vmem),
        scratch_shapes=[
            pltpu.VMEM((comps, LANES, LANES), bf16),
            pltpu.VMEM((degrees, LANES, LANES), bf16),
            pltpu.VMEM((LANES, LANES), bf16),
            pltpu.VMEM((LANES, LANES), bf16),
            pltpu.VMEM((1, ghosts), i32),
            pltpu.VMEM((3, 1, LANES), F32),
            pltpu.VMEM((1, LANES), i32),
            pltpu.VMEM((lists, LANES), i32),
            pltpu.VMEM((degrees, LANES), F32),
            pltpu.VMEM((group, blocks, LANES), F32),
            pltpu.VMEM((3, blocks * LANES), F32),
            pltpu.VMEM((LANES, LANES), bf16),
            pltpu.VMEM((comps + 1, LANES, LANES), bf16),
            pltpu.VMEM((comps + 1, ghosts, LANES), bf16),
            pltpu.VMEM((comps + 1, 8, ghosts, LANES), bf16),
            pltpu.VMEM((table_size, LANES), F32),
            pltpu.VMEM((LANES, table_size), F32),
            pltpu.VMEM((comps, LANES, LANES), F32),
            pltpu.VMEM((group * blocks, LANES, LANES), F32),
            pltpu.VMEM((group * blocks, LANES, LANES), F32),
            pltpu.VMEM((3, LANES, LANES), F32),
            pltpu.VMEM((group, TILE, LANES), F32),
            pltpu.VMEM((group, 1, LANES), F32),
            pltpu.VMEM((5, group, LANES), F32),
            pltpu.VMEM((ITERS, 2, rows, LANES), F32),
            pltpu.VMEM((ITERS, 2, ring - 1, rows, LANES), F32),
            pltpu.VMEM((rows, LANES), F32),
            pltpu.VMEM((6, blocks, LANES), F32),
            pltpu.VMEM((ITERS - 1, group + 1, LANES), F32),
            pltpu.VMEM((ITERS - 1, group - 1, group + 1, LANES), F32),
            pltpu.VMEM((group + 1, LANES), F32),
            pltpu.VMEM((LANES, LANES), F32),
            pltpu.VMEM((group, TILE, LANES), F32),
            pltpu.VMEM((group - 1, TILE, LANES), F32),
            dma((11,)),
            dma,
            dma,
            dma((CHUNKS, 2)),
            dma((ITERS + 2,)),
            dma((ITERS + 2,)),
            dma((2,)),
            dma((ITERS, 2)),
        ],
        compiler_params=pltpu.CompilerParams(
            collective_id=1, has_side_effects=True, vmem_limit_bytes=48 * 1024 * 1024
        ),
    )(
        jnp.transpose(equivariant_embedding[0, 0], (1, 0, 2)),
        degree_channel_mixer,
        attention_source_weights,
        attention_target_weights,
        halo_export_indices[0],
        cartesian_coordinates[0, 0].reshape(3, 1, LANES),
        element_identity[0],
        adjacency_rows[0, 0].T,
        affinity_output_head,
        ewald_weighting.reshape(group, blocks, LANES),
        reciprocal_lattice_points,
        occupied_site_totals,
        baseline_affinity_per_element,
        chemical_stiffness,
    )
    return (charges.reshape(1, 1, LANES), forces.reshape(1, 1, 3, LANES))


def solution(mesh):
    placed = (
        P("dom", "slab", None, None, None),
        P("dom", "slab", None, None),
        P("dom", "slab", None),
        P("dom", "slab"),
        P("dom", "slab", None),
        P("dom", "slab", None, None),
        P(),
        P(),
        P(),
        P(),
        P(),
        P(),
        P(),
        P(),
    )
    return jax.shard_map(
        shards,
        mesh=mesh,
        in_specs=placed,
        out_specs=(P("dom", "slab", None), P("dom", "slab", None, None)),
        check_vma=False,
    )
```

```python
import math

import jax
import jax.numpy as jnp
from jax import lax
from jax.experimental import pallas as pl
from jax.experimental.pallas import tpu as pltpu
from jax.sharding import PartitionSpec as P

ITERS = 4
CHIPS_X = 4
LANES = 128
MESH = pl.DeviceIdType.MESH
F32 = jnp.float32

HALF_PI_PARTS = (1.5703125, 4.837512969970703125e-4, 7.54978995489188216e-8)


def sine_cosine(phase):
    quadrant = jnp.round(phase * (2.0 / math.pi))
    reduced = phase - quadrant * HALF_PI_PARTS[0]
    reduced = reduced - quadrant * HALF_PI_PARTS[1]
    reduced = reduced - quadrant * HALF_PI_PARTS[2]
    square = reduced * reduced
    odd = (-1.9515295891e-4 * square + 8.3321608736e-3) * square - 1.6666654611e-1
    odd = odd * square * reduced + reduced
    even = (2.443315711809948e-5 * square - 1.388731625493765e-3) * square
    even = (even + 4.166664568298827e-2) * square * square - 0.5 * square + 1.0
    turn = quadrant.astype(jnp.int32)
    swap = (turn & 1) == 1
    sine = jnp.where(swap, even, odd)
    cosine = jnp.where(swap, odd, even)
    sine = jnp.where((turn & 2) == 2, -sine, sine)
    cosine = jnp.where(((turn + 1) & 2) == 2, -cosine, cosine)
    return sine, cosine


CHUNKS = 2
BLOCKS = (1, 7, 3, 5, 0, 2, 6, 8)
SCALARS = 3
TILE = 8


def place_of(shape):
    chips_x, chips_y, chips_z = shape
    dom, slab = lax.axis_index("dom"), lax.axis_index("slab")
    return lax.div(dom, chips_z), lax.div(slab, 2), lax.rem(dom, chips_z), lax.rem(slab, 2)


def device(shape, x, y, z, core):
    return (x * shape[2] + z, y * 2 + core)


def far_first(count):
    return sorted(range(1, count), key=lambda j: -min(j, count - j))


def sum_partners(shape):
    x, y, z, core = place_of(shape)
    chips_x, ring, _ = shape
    group = 2 * chips_x
    mine = x * 2 + core
    peers = []
    for i in far_first(group):
        other = lax.rem(mine + i, group)
        peers.append((other, device(shape, lax.div(other, 2), y, z, lax.rem(other, 2))))
    along = [
        device(shape, x, lax.rem(y + j * (1 - core), ring), lax.rem(z + j * core, ring), core)
        for j in far_first(ring)
    ]
    across = [
        device(shape, x, lax.rem(y + j * core, ring), lax.rem(z + j * (1 - core), ring), core)
        for j in far_first(ring)
    ]
    return mine, peers, along, across


def halo_partners(shape):
    x, y, z, core = place_of(shape)
    domains = shape[0] * shape[2]
    dom, slab = lax.axis_index("dom"), lax.axis_index("slab")
    way = 1 - 2 * core
    return {
        "before": (lax.rem(dom + domains - 1, domains), slab),
        "after": (lax.rem(dom + 1, domains), slab),
        "pair": (dom, y * 2 + 1 - core),
        "outer": (dom, lax.rem(slab + 2 * shape[1] - way, 2 * shape[1])),
        "ahead": (lax.rem(dom + domains + way, domains), slab),
    }


def row_of(column, eye):
    return jnp.sum(jnp.where(eye, column, 0.0), axis=0, keepdims=True)


def identity_mask(count):
    shape = (count, count)
    return lax.broadcasted_iota(jnp.int32, shape, 0) == lax.broadcasted_iota(jnp.int32, shape, 1)


def degrees_of(comps):
    return [range(l * l, (l + 1) * (l + 1)) for l in range(math.isqrt(comps))]


def fill_mask(adjacency_ref, upright, mask_ref):
    size = upright.shape[0]
    ghosts = (size - LANES) // 8
    group = 64

    def per_group(part, carry):
        start = part * group
        row = lax.broadcasted_iota(jnp.int32, (group, LANES), 0) + start
        slot = row - LANES
        shift = jnp.zeros_like(row)
        for i, block in enumerate(BLOCKS):
            inside = (slot >= i * ghosts) & (slot < (i + 1) * ghosts)
            shift = jnp.where(inside, (block - i) * ghosts, shift)
        row = row + shift
        hit = row == adjacency_ref[0:1, :]
        for j in range(1, adjacency_ref.shape[0]):
            hit = hit | (row == adjacency_ref[j : j + 1, :])
        upright[pl.ds(pl.multiple_of(start, group), group), :] = jnp.where(hit, 1.0, 0.0)
        return carry

    lax.fori_loop(0, size // group, per_group, 0)
    for part in range(size // LANES):
        span = slice(part * LANES, (part + 1) * LANES)
        mask_ref[:, span] = upright[span, :].T


def attention(queries, keys, mask):
    scores = lax.dot_general(
        queries, keys, (((1,), (1,)), ((), ())), preferred_element_type=F32
    )
    gate = jax.nn.sigmoid(scores / math.sqrt(LANES)) * 0.125
    return jnp.where(mask > 0.0, gate, 0.0).astype(jnp.bfloat16)


def spread(rows):
    return jnp.concatenate([rows] * (LANES // rows.shape[0]), axis=0).T


def wide(columns, index):
    return jnp.broadcast_to(columns[:, index : index + 1], (LANES, LANES))


def fill_tables(first, stop, blocks, waves, about, sites, cos_ref, sin_ref):
    step_rows = 64

    def per_member(member, carry):
        columns = spread(about[member])
        for axis in range(3):
            sites[axis] = wide(columns, axis)

        def per_rows(part, inner):
            block, rows = part // (LANES // step_rows), part % (LANES // step_rows)
            lanes = pl.ds(pl.multiple_of(block * LANES, LANES), LANES)
            rows = pl.ds(pl.multiple_of(rows * step_rows, step_rows), step_rows)
            phase = (
                sites[0, rows, :] * waves[0:1, lanes]
                + sites[1, rows, :] * waves[1:2, lanes]
                + sites[2, rows, :] * waves[2:3, lanes]
            )
            sine, cosine = sine_cosine(phase)
            cos_ref[member * blocks + block, rows, :] = cosine
            sin_ref[member * blocks + block, rows, :] = sine
            return inner

        return lax.fori_loop(0, blocks * LANES // step_rows, per_rows, carry)

    lax.fori_loop(first, stop, per_member, 0)


def whole_kernel(
    shape,
    features_hbm,
    mixer_hbm,
    source_hbm,
    target_hbm,
    export_hbm,
    place_hbm,
    species_hbm,
    adjacency_hbm,
    head_hbm,
    weight_hbm,
    waves_hbm,
    baseline_hbm,
    stiffness_hbm,
    count_ref,
    charges_ref,
    forces_ref,
    features_ref,
    mixer_ref,
    source_ref,
    target_ref,
    export_ref,
    place_ref,
    species_ref,
    adjacency_ref,
    head_ref,
    weight_ref,
    waves,
    baseline_ref,
    stiffness_ref,
    queries,
    table,
    outgoing,
    arrived,
    upright,
    mask_ref,
    own_message,
    cos_ref,
    sin_ref,
    sites,
    about,
    first_rows,
    vectors,
    parts,
    inbox,
    ring_total,
    factors,
    posts,
    post_inbox,
    post_total,
    matrix,
    fields,
    field_inbox,
    load_sem,
    halo_send,
    halo_recv,
    near_recv,
    group_send,
    group_recv,
    ring_send,
    ring_recv,
):
    me, peers, along, across = sum_partners(shape)
    near = halo_partners(shape)
    core = place_of(shape)[3]
    group = len(peers) + 1
    comps = features_ref.shape[0]
    ghosts = outgoing.shape[1]
    blocks = cos_ref.shape[0] // group
    span = blocks * LANES
    scale = 1.0 / math.sqrt(lax.axis_size("dom") * lax.axis_size("slab") * LANES)
    bf16 = jnp.bfloat16

    own_waves = waves_hbm.at[:, pl.ds(pl.multiple_of(me * span, LANES), span)]
    loads = [
        pltpu.make_async_copy(source, target, load_sem.at[i])
        for i, (source, target) in enumerate(
            (
                (features_hbm, features_ref),
                (mixer_hbm, mixer_ref),
                (source_hbm, source_ref),
                (target_hbm, target_ref),
                (export_hbm, export_ref),
                (place_hbm, place_ref),
                (species_hbm, species_ref),
                (adjacency_hbm, adjacency_ref),
                (head_hbm, head_ref),
                (weight_hbm, weight_ref),
                (own_waves, waves),
                (baseline_hbm, baseline_ref),
                (stiffness_hbm, stiffness_ref),
            )
        )
    ]
    for item in loads:
        item.start()
    everyone = [near[name] for name in ("before", "after", "pair", "outer")]
    everyone += [peer for _, peer in peers] + along + across
    barrier = pltpu.get_barrier_semaphore()
    for partner in everyone:
        pl.semaphore_signal(barrier, inc=1, device_id=partner, device_id_type=MESH)
    eye = identity_mask(LANES)

    for i in (5, 6, 11, 12):
        loads[i].wait()
    species = species_ref[...]
    hardness = jnp.zeros(species.shape, F32)
    baseline = jnp.zeros(species.shape, F32)
    for element in range(stiffness_ref.shape[1]):
        here = species == element
        hardness = jnp.where(here, stiffness_ref[0:1, element : element + 1], hardness)
        baseline = jnp.where(here, baseline_ref[0:1, element : element + 1], baseline)
    live = lax.broadcasted_iota(jnp.int32, (1, LANES), 1) < count_ref[0, 0]
    live = jnp.where(live, 1.0, 0.0)
    about[me] = jnp.zeros((TILE, LANES), F32)
    for axis in range(3):
        about[me, axis : axis + 1, :] = place_ref[axis]
    about[me, 3:4, :] = hardness
    about[me, 4:5, :] = live

    for i in range(5):
        loads[i].wait()
    offered = jnp.broadcast_to(export_ref[...], (ghosts, ghosts)).astype(F32)
    offered = jnp.sum(jnp.where(identity_mask(ghosts), offered, 0.0), axis=1, keepdims=True)
    slots = lax.broadcasted_iota(jnp.int32, (ghosts, LANES), 1).astype(F32)
    pick = jnp.where(slots == offered, 1.0, 0.0).astype(bf16)
    size = (comps + 1) // CHUNKS

    def offer(chunk):
        for index in range(chunk * size, (chunk + 1) * size):
            comp = 0 if index == comps else index
            mix = target_ref[...] if index == comps else mixer_ref[math.isqrt(comp)]
            row = jnp.dot(pick, features_ref[comp], preferred_element_type=F32).astype(bf16)
            outgoing[index] = jnp.dot(row, mix, preferred_element_type=F32).astype(bf16)

    pl.semaphore_wait(barrier, len(everyone))

    def ship(chunk, source, slot, target, sem):
        rows = pl.ds(chunk * size, size)
        copy = pltpu.make_async_remote_copy(
            src_ref=source,
            dst_ref=arrived.at[rows, slot],
            send_sem=halo_send,
            recv_sem=sem,
            device_id=target,
            device_id_type=MESH,
        )
        copy.start()

    def own(chunk):
        return outgoing.at[pl.ds(chunk * size, size)]

    def got(chunk, slot):
        return arrived.at[pl.ds(chunk * size, size), slot]

    def all_of(ref, send, receive):
        return pltpu.make_async_remote_copy(
            src_ref=ref,
            dst_ref=ref,
            send_sem=send,
            recv_sem=receive,
            device_id=near["pair"],
            device_id_type=MESH,
        )

    def to_group(pieces, drops, stage):
        for i, (_, target) in enumerate(peers):
            pltpu.make_async_remote_copy(
                src_ref=pieces(i),
                dst_ref=drops(i),
                send_sem=group_send.at[stage],
                recv_sem=group_recv.at[stage],
                device_id=target,
                device_id_type=MESH,
            ).start()

    to_group(lambda i: about.at[me], lambda i: about.at[me], 0)
    for chunk in range(CHUNKS):
        offer(chunk)
        ship(chunk, own(chunk), 0, near["after"], near_recv.at[chunk, 0])
        ship(chunk, own(chunk), 1, near["before"], near_recv.at[chunk, 0])
        ship(chunk, own(chunk), 3 - core, near["outer"], near_recv.at[chunk, 1])
        ship(chunk, own(chunk), 2 + core, near["pair"], near_recv.at[chunk, 2])

    def relay_outer(chunk):
        all_of(got(chunk, 0), halo_send, near_recv.at[chunk, 1]).wait_recv()
        ship(chunk, got(chunk, 2 + core), 4 + 3 * core, near["ahead"], halo_recv)

    def relay_near(chunk):
        both = arrived.at[pl.ds(chunk * size, size), pl.ds(0, 2)]
        all_of(both, halo_send, near_recv.at[chunk, 0]).wait_recv()
        ship(chunk, got(chunk, core), 5 + core, near["outer"], halo_recv)
        ship(chunk, got(chunk, 0), 4 + core, near["pair"], halo_recv)
        ship(chunk, got(chunk, 1), 6 + core, near["pair"], halo_recv)

    def tables_of(first, stop):
        fill_tables(first, stop, blocks, waves, about, sites, cos_ref, sin_ref)

    loads[7].wait()
    fill_mask(adjacency_ref, upright, mask_ref)
    relay_outer(0)
    for degree, members in enumerate(degrees_of(comps)):
        for comp in members:
            product = jnp.dot(
                features_ref[comp], mixer_ref[degree], preferred_element_type=F32
            )
            table[comp] = product.astype(bf16)
    scalar = features_ref[0]
    table[comps] = jnp.dot(scalar, target_ref[...], preferred_element_type=F32).astype(bf16)
    queries[...] = jnp.dot(scalar, source_ref[...], preferred_element_type=F32).astype(bf16)
    for i in range(8, 11):
        loads[i].wait()
    others = about.at[pl.ds(0, group - 1)]
    all_of(others, group_send.at[0], group_recv.at[0]).wait_recv()
    tables_of(0, group // 4)
    relay_near(0)
    relay_outer(1)
    tables_of(group // 4, 3 * group // 4)
    relay_near(1)
    for chunk in range(CHUNKS):
        all_of(got(chunk, 0), halo_send, near_recv.at[chunk, 2]).wait_recv()

    def both_of(comp):
        return jnp.concatenate([table[comp], arrived[comp, 0:4].reshape(4 * ghosts, LANES)], axis=0)

    reach = LANES + 4 * ghosts
    near_weights = attention(queries[...], both_of(comps), mask_ref[:, 0:reach])
    for comp in range(comps):
        own_message[comp] = jnp.dot(near_weights, both_of(comp), preferred_element_type=F32)
    tables_of(3 * group // 4, group)
    for member in range(group):
        vectors[3, member : member + 1, :] = about[member, 3:4, :]
        vectors[4, member : member + 1, :] = about[member, 4:5, :]
    vectors[1] = jnp.zeros((group, LANES), F32)
    vectors[2] = jnp.zeros((group, LANES), F32)
    factors[...] = jnp.zeros_like(factors)
    all_of(arrived.at[:, pl.ds(0, 4)], halo_send, halo_recv).wait_recv()

    far_keys = arrived[comps, 4:8].reshape(4 * ghosts, LANES)
    weights = attention(queries[...], far_keys, mask_ref[:, reach:])
    readout = jnp.zeros((LANES, LANES), F32)
    for degree, members in enumerate(degrees_of(comps)):
        square = jnp.zeros((LANES, LANES), F32)
        for comp in members:
            message = own_message[comp] + jnp.dot(
                weights, arrived[comp, 4:8].reshape(4 * ghosts, LANES), preferred_element_type=F32
            )
            square = message if degree == 0 else square + message * message
        norm = square if degree == 0 else jnp.sqrt(square + 1e-06)
        readout = readout + norm * head_ref[degree : degree + 1, :]
    electroneg = row_of(jnp.sum(readout, axis=1, keepdims=True), eye) + baseline
    first_rows[me] = -electroneg * live
    to_group(lambda i: first_rows.at[me], lambda i: first_rows.at[me], 1)
    starts = first_rows.at[pl.ds(0, group - 1)]
    all_of(starts, group_send.at[1], group_recv.at[1]).wait_recv()
    for member in range(group):
        vectors[0, member : member + 1, :] = first_rows[member]

    lanes = lax.broadcasted_iota(jnp.int32, (LANES, LANES), 1)
    scalar_row = 2 * blocks
    weight = weight_ref[me]
    tables = (cos_ref, sin_ref)

    def full_sum(rows):
        return jnp.sum(jnp.sum(rows, axis=0, keepdims=True), axis=1, keepdims=True)

    def project(turn):
        residual = vectors[0]
        columns = spread(residual)
        sums = [[jnp.zeros((TILE, LANES), F32) for _ in range(blocks)] for _ in range(2)]
        for member in range(group):
            column = wide(columns, member)
            for part in range(2):
                for block in range(blocks):
                    product = tables[part][member * blocks + block] * column
                    product = product.reshape(LANES // TILE, TILE, LANES)
                    sums[part][block] = sums[part][block] + jnp.sum(product, axis=0)
        for part in range(2):
            for block in range(blocks):
                row = part * blocks + block
                parts[turn, 0, row : row + 1, :] = jnp.sum(
                    sums[part][block], axis=0, keepdims=True
                )
        hard_residual = vectors[3] * residual
        scalars = (residual * residual, hard_residual * residual, hard_residual * vectors[1])
        for i, product in enumerate(scalars):
            row = scalar_row + i
            parts[turn, 0, row : row + 1, :] = jnp.broadcast_to(full_sum(product), (1, LANES))

    def ring_stage(turn, stage):
        sems = (ring_send.at[turn, stage], ring_recv.at[turn, stage])
        return all_of(inbox.at[turn, stage], *sems)

    def post_stage(turn):
        return all_of(post_inbox.at[turn], group_send.at[2 + turn], group_recv.at[2 + turn])

    def ring_sum(turn, meanwhile):
        held = parts[turn, 0]
        for stage, targets in enumerate((along, across)):
            if stage > 0:
                parts[turn, stage] = held
            for i, target in enumerate(targets):
                pltpu.make_async_remote_copy(
                    src_ref=parts.at[turn, stage],
                    dst_ref=inbox.at[turn, stage, i],
                    send_sem=ring_send.at[turn, stage],
                    recv_sem=ring_recv.at[turn, stage],
                    device_id=target,
                    device_id_type=MESH,
                ).start()
            if stage == 0:
                meanwhile()
            ring_stage(turn, stage).wait_recv()
            for i in range(len(targets)):
                held = held + inbox[turn, stage, i]
        ring_total[...] = held

    def follow(turn, previous_norm, stiff_part):
        norm, pure, mixed = (
            ring_total[scalar_row + i : scalar_row + i + 1, :] for i in range(SCALARS)
        )
        beta = jnp.where(turn > 0, norm / previous_norm, 0.0)
        stiff_part = pure + 2.0 * beta * mixed + beta * beta * stiff_part
        recip = jnp.zeros_like(weight)
        for part in range(2):
            rows = ring_total[part * blocks : (part + 1) * blocks, :] + beta * factors[part]
            factors[part] = rows
            factors[2 + part] = weight * rows
            recip = recip + weight * rows * rows
        vectors[1] = vectors[0] + beta * vectors[1]
        return norm, stiff_part, jnp.broadcast_to(full_sum(recip), (1, LANES))

    def iteration(turn, carry):
        project(turn)
        ring_sum(turn, lambda: None)
        norm, stiff_part, recip = follow(turn, *carry)

        def back(step, acc):
            for j in range(2):
                member = 2 * step + j
                image = jnp.zeros((LANES, LANES), F32)
                for block in range(blocks):
                    for part in range(2):
                        row = factors[2 + part, block : block + 1, :]
                        image = image + tables[part][member * blocks + block] * row
                acc = jnp.where(lanes == member, jnp.sum(image, axis=1, keepdims=True), acc)
            return acc

        images = lax.fori_loop(0, group // 2, back, jnp.zeros((LANES, LANES), F32))
        posts[turn, 0:group, :] = images.T[0:group, :]
        posts[turn, group : group + 1, :] = recip
        to_group(lambda i: posts.at[turn], lambda i: post_inbox.at[turn, i], 2 + turn)
        held = posts[turn]
        post_stage(turn).wait_recv()
        for i in range(group - 1):
            held = held + post_inbox[turn, i]
        post_total[...] = held
        step = norm / (stiff_part + scale * post_total[group : group + 1, :])
        direction = vectors[1]
        image = vectors[4] * (vectors[3] * direction + scale * post_total[0:group, :])
        vectors[2] = vectors[2] + step * direction
        vectors[0] = vectors[0] - step * image
        for part in range(2):
            factors[4 + part] = factors[4 + part] + step * factors[2 + part]
        return norm, stiff_part

    def field_of(first, offset):
        half = LANES // 2

        def per_pair(step, carry):
            for part in range(4):
                member = 2 * step + part // 2
                rows = pl.ds(part % 2 * half, half)
                sums = [jnp.zeros((half, LANES), F32) for _ in range(3)]
                for block in range(blocks):
                    where = member * blocks + block
                    term = (
                        sin_ref[where, rows, :] * factors[first, block : block + 1, :]
                        - cos_ref[where, rows, :] * factors[first + 1, block : block + 1, :]
                    )
                    for axis in range(3):
                        wave = waves[axis : axis + 1, block * LANES : (block + 1) * LANES]
                        sums[axis] = sums[axis] + term * wave
                filled = matrix[rows, :]
                for axis in range(3):
                    column = jnp.sum(sums[axis], axis=1, keepdims=True)
                    place = member * TILE + offset + axis
                    filled = jnp.where(lanes[0:half, :] == place, column, filled)
                matrix[rows, :] = filled
            return carry

        lax.fori_loop(0, group // 2, per_pair, 0)

    ones = jnp.ones((1, LANES), F32)
    carry = lax.fori_loop(0, ITERS - 1, iteration, (ones, ones))

    turn = ITERS - 1
    matrix[...] = jnp.zeros_like(matrix)
    project(turn)
    ring_sum(turn, lambda: field_of(4, 0))
    norm, stiff_part, recip = follow(turn, *carry)
    field_of(2, 3)
    field_rows = matrix[...].T
    for member in range(group):
        fields[member] = field_rows[member * TILE : (member + 1) * TILE, :]
        fields[member, 6:7, :] = recip
    stage = 1 + ITERS
    to_group(lambda i: fields.at[peers[i][0]], lambda i: field_inbox.at[i], stage)
    held = fields[me]
    all_of(arrived, halo_send, halo_recv).wait_send()
    all_of(others, group_send.at[0], group_recv.at[0]).wait_send()
    all_of(starts, group_send.at[1], group_recv.at[1]).wait_send()
    for sent in range(ITERS):
        ring_stage(sent, 0).wait_send()
        ring_stage(sent, 1).wait_send()
        if sent < turn:
            post_stage(sent).wait_send()
    all_of(field_inbox, group_send.at[stage], group_recv.at[stage]).wait()
    for i in range(group - 1):
        held = held + field_inbox[i]
    fields[me] = held
    step = norm / (stiff_part + scale * fields[me, 6:7, :])
    vectors[2] = vectors[2] + step * vectors[1]
    charges = vectors[2, pl.ds(me, 1), :]
    charges_ref[...] = charges
    for axis in range(3):
        field = fields[me, axis : axis + 1, :] + step * fields[me, 3 + axis : 4 + axis, :]
        forces_ref[axis] = charges * (scale * field)


def shards(
    equivariant_embedding,
    cartesian_coordinates,
    element_identity,
    occupied_site_totals,
    halo_export_indices,
    adjacency_rows,
    attention_source_weights,
    attention_target_weights,
    degree_channel_mixer,
    affinity_output_head,
    baseline_affinity_per_element,
    chemical_stiffness,
    reciprocal_lattice_points,
    ewald_weighting,
):
    chips_x = CHIPS_X
    ring = lax.axis_size("slab") // 2
    shape = (chips_x, ring, lax.axis_size("dom") // chips_x)
    assert shape[1] == shape[2]
    comps = equivariant_embedding.shape[3]
    ghosts = halo_export_indices.shape[2]
    degrees = degree_channel_mixer.shape[0]
    lists = adjacency_rows.shape[3]
    elements = chemical_stiffness.shape[0]
    group = 2 * chips_x
    blocks = reciprocal_lattice_points.shape[1] // LANES // group
    rows = 2 * blocks + SCALARS
    table_size = LANES + 8 * ghosts
    bf16, i32 = jnp.bfloat16, jnp.int32
    assert group * TILE <= LANES and (comps + 1) % CHUNKS == 0
    vmem = pl.BlockSpec(memory_space=pltpu.VMEM)
    smem = pl.BlockSpec(memory_space=pltpu.SMEM)
    hbm = pl.BlockSpec(memory_space=pltpu.HBM)
    dma = pltpu.SemaphoreType.DMA
    operands = (
        jnp.transpose(equivariant_embedding[0, 0], (1, 0, 2)),
        degree_channel_mixer,
        attention_source_weights,
        attention_target_weights,
        halo_export_indices[0],
        cartesian_coordinates[0, 0].reshape(3, 1, LANES),
        element_identity[0],
        adjacency_rows[0, 0].T,
        affinity_output_head,
        ewald_weighting.reshape(group, blocks, LANES),
        reciprocal_lattice_points,
        baseline_affinity_per_element.reshape(1, elements),
        chemical_stiffness.reshape(1, elements),
    )
    charges, forces = pl.pallas_call(
        lambda *refs: whole_kernel(shape, *refs),
        name="equilibrate",
        out_shape=(
            jax.ShapeDtypeStruct((1, LANES), F32),
            jax.ShapeDtypeStruct((3, 1, LANES), F32),
        ),
        in_specs=[hbm] * 13 + [smem],
        out_specs=(vmem, vmem),
        scratch_shapes=[
            pltpu.VMEM((comps, LANES, LANES), bf16),
            pltpu.VMEM((degrees, LANES, LANES), bf16),
            pltpu.VMEM((LANES, LANES), bf16),
            pltpu.VMEM((LANES, LANES), bf16),
            pltpu.VMEM((1, ghosts), i32),
            pltpu.VMEM((3, 1, LANES), F32),
            pltpu.VMEM((1, LANES), i32),
            pltpu.VMEM((lists, LANES), i32),
            pltpu.VMEM((degrees, LANES), F32),
            pltpu.VMEM((group, blocks, LANES), F32),
            pltpu.VMEM((3, blocks * LANES), F32),
            pltpu.VMEM((1, elements), F32),
            pltpu.VMEM((1, elements), F32),
            pltpu.VMEM((LANES, LANES), bf16),
            pltpu.VMEM((comps + 1, LANES, LANES), bf16),
            pltpu.VMEM((comps + 1, ghosts, LANES), bf16),
            pltpu.VMEM((comps + 1, 8, ghosts, LANES), bf16),
            pltpu.VMEM((table_size, LANES), F32),
            pltpu.VMEM((LANES, table_size), F32),
            pltpu.VMEM((comps, LANES, LANES), F32),
            pltpu.VMEM((group * blocks, LANES, LANES), F32),
            pltpu.VMEM((group * blocks, LANES, LANES), F32),
            pltpu.VMEM((3, LANES, LANES), F32),
            pltpu.VMEM((group, TILE, LANES), F32),
            pltpu.VMEM((group, 1, LANES), F32),
            pltpu.VMEM((5, group, LANES), F32),
            pltpu.VMEM((ITERS, 2, rows, LANES), F32),
            pltpu.VMEM((ITERS, 2, ring - 1, rows, LANES), F32),
            pltpu.VMEM((rows, LANES), F32),
            pltpu.VMEM((6, blocks, LANES), F32),
            pltpu.VMEM((ITERS - 1, group + 1, LANES), F32),
            pltpu.VMEM((ITERS - 1, group - 1, group + 1, LANES), F32),
            pltpu.VMEM((group + 1, LANES), F32),
            pltpu.VMEM((LANES, LANES), F32),
            pltpu.VMEM((group, TILE, LANES), F32),
            pltpu.VMEM((group - 1, TILE, LANES), F32),
            dma((13,)),
            dma,
            dma,
            dma((CHUNKS, 3)),
            dma((ITERS + 2,)),
            dma((ITERS + 2,)),
            dma((ITERS, 2)),
            dma((ITERS, 2)),
        ],
        compiler_params=pltpu.CompilerParams(
            collective_id=1, has_side_effects=True, vmem_limit_bytes=48 * 1024 * 1024
        ),
    )(*(pltpu.with_memory_space_constraint(item, pltpu.HBM) for item in operands), occupied_site_totals)
    return (charges.reshape(1, 1, LANES), forces.reshape(1, 1, 3, LANES))


def solution(mesh):
    placed = (
        P("dom", "slab", None, None, None),
        P("dom", "slab", None, None),
        P("dom", "slab", None),
        P("dom", "slab"),
        P("dom", "slab", None),
        P("dom", "slab", None, None),
        P(),
        P(),
        P(),
        P(),
        P(),
        P(),
        P(),
        P(),
    )
    return jax.shard_map(
        shards,
        mesh=mesh,
        in_specs=placed,
        out_specs=(P("dom", "slab", None), P("dom", "slab", None, None)),
        check_vma=False,
    )
```

```python
import math

import jax
import jax.numpy as jnp
from jax import lax
from jax.experimental import pallas as pl
from jax.experimental.pallas import tpu as pltpu
from jax.sharding import PartitionSpec as P

ITERS = 4
CHIPS_X = 4
LANES = 128
MESH = pl.DeviceIdType.MESH
F32 = jnp.float32

HALF_PI_PARTS = (1.5703125, 4.837512969970703125e-4, 7.54978995489188216e-8)


def sine_cosine(phase):
    quadrant = jnp.round(phase * (2.0 / math.pi))
    reduced = phase - quadrant * HALF_PI_PARTS[0]
    reduced = reduced - quadrant * HALF_PI_PARTS[1]
    reduced = reduced - quadrant * HALF_PI_PARTS[2]
    square = reduced * reduced
    odd = (-1.9515295891e-4 * square + 8.3321608736e-3) * square - 1.6666654611e-1
    odd = odd * square * reduced + reduced
    even = (2.443315711809948e-5 * square - 1.388731625493765e-3) * square
    even = (even + 4.166664568298827e-2) * square * square - 0.5 * square + 1.0
    turn = quadrant.astype(jnp.int32)
    swap = (turn & 1) == 1
    sine = jnp.where(swap, even, odd)
    cosine = jnp.where(swap, odd, even)
    sine = jnp.where((turn & 2) == 2, -sine, sine)
    cosine = jnp.where(((turn + 1) & 2) == 2, -cosine, cosine)
    return sine, cosine


CHUNKS = ((0, 13), (13, 8), (21, 5))
BLOCKS = (1, 7, 3, 5, 0, 2, 6, 8)
SCALARS = 3
TILE = 8


def place_of(shape):
    chips_x, chips_y, chips_z = shape
    dom, slab = lax.axis_index("dom"), lax.axis_index("slab")
    return lax.div(dom, chips_z), lax.div(slab, 2), lax.rem(dom, chips_z), lax.rem(slab, 2)


def device(shape, x, y, z, core):
    return (x * shape[2] + z, y * 2 + core)


def far_first(count):
    return sorted(range(1, count), key=lambda j: -min(j, count - j))


def sum_partners(shape):
    x, y, z, core = place_of(shape)
    chips_x, ring, _ = shape
    mine = x * 2 + core
    peers = []
    steps = [(dx, dc) for dx in far_first(chips_x) for dc in (0, 1)] + [(0, 1)]
    for dx, dc in steps:
        other_x, other_core = lax.rem(x + dx, chips_x), lax.rem(core + dc, 2)
        peers.append((other_x * 2 + other_core, device(shape, other_x, y, z, other_core)))
    along = [
        device(shape, x, lax.rem(y + j * (1 - core), ring), lax.rem(z + j * core, ring), core)
        for j in far_first(ring)
    ]
    across = [
        device(shape, x, lax.rem(y + j * core, ring), lax.rem(z + j * (1 - core), ring), core)
        for j in far_first(ring)
    ]
    return mine, peers, along, across


def halo_partners(shape):
    x, y, z, core = place_of(shape)
    domains = shape[0] * shape[2]
    dom, slab = lax.axis_index("dom"), lax.axis_index("slab")
    way = 1 - 2 * core
    return {
        "before": (lax.rem(dom + domains - 1, domains), slab),
        "after": (lax.rem(dom + 1, domains), slab),
        "pair": (dom, y * 2 + 1 - core),
        "outer": (dom, lax.rem(slab + 2 * shape[1] - way, 2 * shape[1])),
        "ahead": (lax.rem(dom + domains + way, domains), slab),
    }


def row_of(column, eye):
    return jnp.sum(jnp.where(eye, column, 0.0), axis=0, keepdims=True)


def identity_mask(count):
    shape = (count, count)
    return lax.broadcasted_iota(jnp.int32, shape, 0) == lax.broadcasted_iota(jnp.int32, shape, 1)


def degrees_of(comps):
    return [range(l * l, (l + 1) * (l + 1)) for l in range(math.isqrt(comps))]


def fill_mask(adjacency_ref, upright, mask_ref):
    size = upright.shape[0]
    ghosts = (size - LANES) // 8
    group = 64

    def per_group(part, carry):
        start = part * group
        row = lax.broadcasted_iota(jnp.int32, (group, LANES), 0) + start
        slot = row - LANES
        shift = jnp.zeros_like(row)
        for i, block in enumerate(BLOCKS):
            inside = (slot >= i * ghosts) & (slot < (i + 1) * ghosts)
            shift = jnp.where(inside, (block - i) * ghosts, shift)
        row = row + shift
        hit = row == adjacency_ref[0:1, :]
        for j in range(1, adjacency_ref.shape[0]):
            hit = hit | (row == adjacency_ref[j : j + 1, :])
        upright[pl.ds(pl.multiple_of(start, group), group), :] = jnp.where(hit, 1.0, 0.0)
        return carry

    lax.fori_loop(0, size // group, per_group, 0)
    for part in range(size // LANES):
        span = slice(part * LANES, (part + 1) * LANES)
        mask_ref[:, span] = upright[span, :].T


def attention(queries, keys, mask):
    scores = lax.dot_general(
        queries, keys, (((1,), (1,)), ((), ())), preferred_element_type=F32
    )
    gate = jax.nn.sigmoid(scores / math.sqrt(LANES)) * 0.125
    return jnp.where(mask > 0.0, gate, 0.0).astype(jnp.bfloat16)


def spread(rows):
    return jnp.concatenate([rows] * (LANES // rows.shape[0]), axis=0).T


def wide(columns, index):
    return jnp.broadcast_to(columns[:, index : index + 1], (LANES, LANES))


def fill_tables(first, stop, blocks, waves, about, sites, cos_ref, sin_ref):
    step_rows = 64

    def per_member(member, carry):
        columns = spread(about[member])
        for axis in range(3):
            sites[axis] = wide(columns, axis)

        def per_rows(part, inner):
            block, rows = part // (LANES // step_rows), part % (LANES // step_rows)
            lanes = pl.ds(pl.multiple_of(block * LANES, LANES), LANES)
            rows = pl.ds(pl.multiple_of(rows * step_rows, step_rows), step_rows)
            phase = (
                sites[0, rows, :] * waves[0:1, lanes]
                + sites[1, rows, :] * waves[1:2, lanes]
                + sites[2, rows, :] * waves[2:3, lanes]
            )
            sine, cosine = sine_cosine(phase)
            cos_ref[member * blocks + block, rows, :] = cosine
            sin_ref[member * blocks + block, rows, :] = sine
            return inner

        return lax.fori_loop(0, blocks * LANES // step_rows, per_rows, carry)

    lax.fori_loop(first, stop, per_member, 0)


def whole_kernel(
    shape,
    features_hbm,
    mixer_hbm,
    source_hbm,
    target_hbm,
    export_hbm,
    place_hbm,
    species_hbm,
    adjacency_hbm,
    head_hbm,
    weight_hbm,
    waves_hbm,
    baseline_hbm,
    stiffness_hbm,
    count_ref,
    charges_ref,
    forces_ref,
    features_ref,
    mixer_ref,
    source_ref,
    target_ref,
    export_ref,
    place_ref,
    species_ref,
    adjacency_ref,
    head_ref,
    weight_ref,
    waves,
    baseline_ref,
    stiffness_ref,
    queries,
    table,
    outgoing,
    arrived,
    upright,
    mask_ref,
    own_message,
    cos_ref,
    sin_ref,
    sites,
    about,
    first_rows,
    vectors,
    parts,
    inbox,
    ring_total,
    factors,
    posts,
    post_inbox,
    post_total,
    matrix,
    fields,
    field_inbox,
    load_sem,
    halo_send,
    halo_recv,
    near_recv,
    group_send,
    group_recv,
    ring_send,
    ring_recv,
):
    me, peers, along, across = sum_partners(shape)
    near = halo_partners(shape)
    core = place_of(shape)[3]
    group = len(peers) + 1
    comps = features_ref.shape[0]
    ghosts = outgoing.shape[1]
    blocks = cos_ref.shape[0] // group
    span = blocks * LANES
    scale = 1.0 / math.sqrt(lax.axis_size("dom") * lax.axis_size("slab") * LANES)
    bf16 = jnp.bfloat16

    own_waves = waves_hbm.at[:, pl.ds(pl.multiple_of(me * span, LANES), span)]
    loads = [
        pltpu.make_async_copy(source, target, load_sem.at[i])
        for i, (source, target) in enumerate(
            (
                (features_hbm, features_ref),
                (mixer_hbm, mixer_ref),
                (source_hbm, source_ref),
                (target_hbm, target_ref),
                (export_hbm, export_ref),
                (place_hbm, place_ref),
                (species_hbm, species_ref),
                (adjacency_hbm, adjacency_ref),
                (head_hbm, head_ref),
                (weight_hbm, weight_ref),
                (own_waves, waves),
                (baseline_hbm, baseline_ref),
                (stiffness_hbm, stiffness_ref),
            )
        )
    ]
    for item in loads:
        item.start()
    everyone = [near[name] for name in ("before", "after", "pair", "outer")]
    everyone += [peer for _, peer in peers] + along + across
    barrier = pltpu.get_barrier_semaphore()
    for partner in everyone:
        pl.semaphore_signal(barrier, inc=1, device_id=partner, device_id_type=MESH)
    eye = identity_mask(LANES)

    for i in (5, 6, 11, 12):
        loads[i].wait()
    species = species_ref[...]
    hardness = jnp.zeros(species.shape, F32)
    baseline = jnp.zeros(species.shape, F32)
    for element in range(stiffness_ref.shape[1]):
        here = species == element
        hardness = jnp.where(here, stiffness_ref[0:1, element : element + 1], hardness)
        baseline = jnp.where(here, baseline_ref[0:1, element : element + 1], baseline)
    live = lax.broadcasted_iota(jnp.int32, (1, LANES), 1) < count_ref[0, 0]
    live = jnp.where(live, 1.0, 0.0)
    about[me] = jnp.zeros((TILE, LANES), F32)
    for axis in range(3):
        about[me, axis : axis + 1, :] = place_ref[axis]
    about[me, 3:4, :] = hardness
    about[me, 4:5, :] = live

    for i in range(5):
        loads[i].wait()
    offered = jnp.broadcast_to(export_ref[...], (ghosts, ghosts)).astype(F32)
    offered = jnp.sum(jnp.where(identity_mask(ghosts), offered, 0.0), axis=1, keepdims=True)
    slots = lax.broadcasted_iota(jnp.int32, (ghosts, LANES), 1).astype(F32)
    pick = jnp.where(slots == offered, 1.0, 0.0).astype(bf16)
    def offer(chunk):
        for index in range(CHUNKS[chunk][0], sum(CHUNKS[chunk])):
            comp = 0 if index == comps else index
            mix = target_ref[...] if index == comps else mixer_ref[math.isqrt(comp)]
            row = jnp.dot(pick, features_ref[comp], preferred_element_type=F32).astype(bf16)
            outgoing[index] = jnp.dot(row, mix, preferred_element_type=F32).astype(bf16)

    pl.semaphore_wait(barrier, len(everyone))

    def ship(chunk, source, slot, target, sem):
        rows = pl.ds(*CHUNKS[chunk])
        copy = pltpu.make_async_remote_copy(
            src_ref=source,
            dst_ref=arrived.at[rows, slot],
            send_sem=halo_send,
            recv_sem=sem,
            device_id=target,
            device_id_type=MESH,
        )
        copy.start()

    def own(chunk):
        return outgoing.at[pl.ds(*CHUNKS[chunk])]

    def got(chunk, slot):
        return arrived.at[pl.ds(*CHUNKS[chunk]), slot]

    def all_of(ref, send, receive):
        return pltpu.make_async_remote_copy(
            src_ref=ref,
            dst_ref=ref,
            send_sem=send,
            recv_sem=receive,
            device_id=near["pair"],
            device_id_type=MESH,
        )

    def to_group(pieces, drops, stage):
        for i, (_, target) in enumerate(peers):
            pltpu.make_async_remote_copy(
                src_ref=pieces(i),
                dst_ref=drops(i),
                send_sem=group_send.at[stage],
                recv_sem=group_recv.at[stage],
                device_id=target,
                device_id_type=MESH,
            ).start()

    to_group(lambda i: about.at[me], lambda i: about.at[me], 0)
    for chunk in range(len(CHUNKS)):
        offer(chunk)
        ship(chunk, own(chunk), 0, near["after"], near_recv.at[chunk, 0])
        ship(chunk, own(chunk), 1, near["before"], near_recv.at[chunk, 0])
        ship(chunk, own(chunk), 3 - core, near["outer"], near_recv.at[chunk, 1])
        ship(chunk, own(chunk), 2 + core, near["pair"], near_recv.at[chunk, 2])

    def relay_outer(chunk):
        all_of(got(chunk, 0), halo_send, near_recv.at[chunk, 1]).wait_recv()
        ship(chunk, got(chunk, 2 + core), 4 + 3 * core, near["ahead"], halo_recv)

    def relay_near(chunk):
        both = arrived.at[pl.ds(*CHUNKS[chunk]), pl.ds(0, 2)]
        all_of(both, halo_send, near_recv.at[chunk, 0]).wait_recv()
        ship(chunk, got(chunk, core), 5 + core, near["outer"], halo_recv)
        ship(chunk, got(chunk, 0), 4 + core, near["pair"], halo_recv)
        ship(chunk, got(chunk, 1), 6 + core, near["pair"], halo_recv)

    def tables_of(first, stop):
        fill_tables(first, stop, blocks, waves, about, sites, cos_ref, sin_ref)

    loads[7].wait()
    fill_mask(adjacency_ref, upright, mask_ref)
    relay_outer(0)
    for degree, members in enumerate(degrees_of(comps)):
        for comp in members:
            product = jnp.dot(
                features_ref[comp], mixer_ref[degree], preferred_element_type=F32
            )
            table[comp] = product.astype(bf16)
    scalar = features_ref[0]
    table[comps] = jnp.dot(scalar, target_ref[...], preferred_element_type=F32).astype(bf16)
    queries[...] = jnp.dot(scalar, source_ref[...], preferred_element_type=F32).astype(bf16)
    for i in range(8, 11):
        loads[i].wait()
    others = about.at[pl.ds(0, group - 1)]
    all_of(others, group_send.at[0], group_recv.at[0]).wait_recv()
    tables_of(0, group // 4)
    relay_near(0)
    relay_outer(1)
    tables_of(group // 4, group // 2)
    relay_near(1)
    relay_outer(2)
    tables_of(group // 2, 5 * group // 8)
    relay_near(2)
    for chunk in range(len(CHUNKS)):
        all_of(got(chunk, 0), halo_send, near_recv.at[chunk, 2]).wait_recv()

    def both_of(comp):
        return jnp.concatenate([table[comp], arrived[comp, 0:4].reshape(4 * ghosts, LANES)], axis=0)

    reach = LANES + 4 * ghosts
    near_weights = attention(queries[...], both_of(comps), mask_ref[:, 0:reach])
    for comp in range(comps):
        own_message[comp] = jnp.dot(near_weights, both_of(comp), preferred_element_type=F32)
    tables_of(5 * group // 8, group)
    for member in range(group):
        vectors[3, member : member + 1, :] = about[member, 3:4, :]
        vectors[4, member : member + 1, :] = about[member, 4:5, :]
    vectors[1] = jnp.zeros((group, LANES), F32)
    vectors[2] = jnp.zeros((group, LANES), F32)
    factors[...] = jnp.zeros_like(factors)
    all_of(arrived.at[:, pl.ds(0, 4)], halo_send, halo_recv).wait_recv()

    far_keys = arrived[comps, 4:8].reshape(4 * ghosts, LANES)
    weights = attention(queries[...], far_keys, mask_ref[:, reach:])
    readout = jnp.zeros((LANES, LANES), F32)
    for degree, members in enumerate(degrees_of(comps)):
        square = jnp.zeros((LANES, LANES), F32)
        for comp in members:
            message = own_message[comp] + jnp.dot(
                weights, arrived[comp, 4:8].reshape(4 * ghosts, LANES), preferred_element_type=F32
            )
            square = message if degree == 0 else square + message * message
        norm = square if degree == 0 else jnp.sqrt(square + 1e-06)
        readout = readout + norm * head_ref[degree : degree + 1, :]
    electroneg = row_of(jnp.sum(readout, axis=1, keepdims=True), eye) + baseline
    first_rows[me] = -electroneg * live
    to_group(lambda i: first_rows.at[me], lambda i: first_rows.at[me], 1)
    starts = first_rows.at[pl.ds(0, group - 1)]
    all_of(starts, group_send.at[1], group_recv.at[1]).wait_recv()
    for member in range(group):
        vectors[0, member : member + 1, :] = first_rows[member]

    lanes = lax.broadcasted_iota(jnp.int32, (LANES, LANES), 1)
    scalar_row = 2 * blocks
    weight = weight_ref[me]
    tables = (cos_ref, sin_ref)

    def full_sum(rows):
        return jnp.sum(jnp.sum(rows, axis=0, keepdims=True), axis=1, keepdims=True)

    def project(turn):
        residual = vectors[0]
        columns = spread(residual)
        sums = [[jnp.zeros((TILE, LANES), F32) for _ in range(blocks)] for _ in range(2)]
        for member in range(group):
            column = wide(columns, member)
            for part in range(2):
                for block in range(blocks):
                    product = tables[part][member * blocks + block] * column
                    product = product.reshape(LANES // TILE, TILE, LANES)
                    sums[part][block] = sums[part][block] + jnp.sum(product, axis=0)
        for part in range(2):
            for block in range(blocks):
                row = part * blocks + block
                parts[turn, 0, row : row + 1, :] = jnp.sum(
                    sums[part][block], axis=0, keepdims=True
                )
        hard_residual = vectors[3] * residual
        scalars = (residual * residual, hard_residual * residual, hard_residual * vectors[1])
        row = jnp.zeros((1, LANES), F32)
        for i, product in enumerate(scalars):
            row = jnp.where(lanes[0:1, :] == i, full_sum(product), row)
        parts[turn, 0, scalar_row : scalar_row + 1, :] = row

    def ring_stage(turn, stage):
        sems = (ring_send.at[turn, stage], ring_recv.at[turn, stage])
        return all_of(inbox.at[turn, stage], *sems)

    def post_stage(turn):
        return all_of(post_inbox.at[turn], group_send.at[2 + turn], group_recv.at[2 + turn])

    def ring_sum(turn, meanwhile):
        held = parts[turn, 0]
        for stage, targets in enumerate((along, across)):
            if stage > 0:
                parts[turn, stage] = held
            for i, target in enumerate(targets):
                pltpu.make_async_remote_copy(
                    src_ref=parts.at[turn, stage],
                    dst_ref=inbox.at[turn, stage, i],
                    send_sem=ring_send.at[turn, stage],
                    recv_sem=ring_recv.at[turn, stage],
                    device_id=target,
                    device_id_type=MESH,
                ).start()
            if stage == 0:
                meanwhile()
            ring_stage(turn, stage).wait_recv()
            for i in range(len(targets)):
                held = held + inbox[turn, stage, i]
        ring_total[...] = held

    def follow(turn, previous_norm, stiff_part):
        norm, pure, mixed = (
            jnp.broadcast_to(ring_total[scalar_row : scalar_row + 1, i : i + 1], (1, LANES))
            for i in range(SCALARS)
        )
        beta = jnp.where(turn > 0, norm / previous_norm, 0.0)
        stiff_part = pure + 2.0 * beta * mixed + beta * beta * stiff_part
        recip = jnp.zeros_like(weight)
        for part in range(2):
            rows = ring_total[part * blocks : (part + 1) * blocks, :] + beta * factors[part]
            factors[part] = rows
            factors[2 + part] = weight * rows
            recip = recip + weight * rows * rows
        vectors[1] = vectors[0] + beta * vectors[1]
        return norm, stiff_part, jnp.broadcast_to(full_sum(recip), (1, LANES))

    def iteration(turn, carry):
        project(turn)
        ring_sum(turn, lambda: None)
        norm, stiff_part, recip = follow(turn, *carry)

        def back(step, acc):
            for j in range(2):
                member = 2 * step + j
                image = jnp.zeros((LANES, LANES), F32)
                for block in range(blocks):
                    for part in range(2):
                        row = factors[2 + part, block : block + 1, :]
                        image = image + tables[part][member * blocks + block] * row
                acc = jnp.where(lanes == member, jnp.sum(image, axis=1, keepdims=True), acc)
            return acc

        images = lax.fori_loop(0, group // 2, back, jnp.zeros((LANES, LANES), F32))
        posts[turn, 0:group, :] = images.T[0:group, :]
        posts[turn, group : group + 1, :] = recip
        to_group(lambda i: posts.at[turn], lambda i: post_inbox.at[turn, i], 2 + turn)
        held = posts[turn]
        post_stage(turn).wait_recv()
        for i in range(group - 1):
            held = held + post_inbox[turn, i]
        post_total[...] = held
        step = norm / (stiff_part + scale * post_total[group : group + 1, :])
        direction = vectors[1]
        image = vectors[4] * (vectors[3] * direction + scale * post_total[0:group, :])
        vectors[2] = vectors[2] + step * direction
        vectors[0] = vectors[0] - step * image
        for part in range(2):
            factors[4 + part] = factors[4 + part] + step * factors[2 + part]
        return norm, stiff_part

    def field_of(first, offset):
        half = LANES // 2

        def per_pair(step, carry):
            for part in range(4):
                member = 2 * step + part // 2
                rows = pl.ds(part % 2 * half, half)
                sums = [jnp.zeros((half, LANES), F32) for _ in range(3)]
                for block in range(blocks):
                    where = member * blocks + block
                    term = (
                        sin_ref[where, rows, :] * factors[first, block : block + 1, :]
                        - cos_ref[where, rows, :] * factors[first + 1, block : block + 1, :]
                    )
                    for axis in range(3):
                        wave = waves[axis : axis + 1, block * LANES : (block + 1) * LANES]
                        sums[axis] = sums[axis] + term * wave
                filled = matrix[rows, :]
                for axis in range(3):
                    column = jnp.sum(sums[axis], axis=1, keepdims=True)
                    place = member * TILE + offset + axis
                    filled = jnp.where(lanes[0:half, :] == place, column, filled)
                matrix[rows, :] = filled
            return carry

        lax.fori_loop(0, group // 2, per_pair, 0)

    ones = jnp.ones((1, LANES), F32)
    carry = lax.fori_loop(0, ITERS - 1, iteration, (ones, ones))

    turn = ITERS - 1
    matrix[...] = jnp.zeros_like(matrix)
    project(turn)
    ring_sum(turn, lambda: field_of(4, 0))
    norm, stiff_part, recip = follow(turn, *carry)
    field_of(2, 3)
    field_rows = matrix[...].T
    for member in range(group):
        fields[member] = field_rows[member * TILE : (member + 1) * TILE, :]
        fields[member, 6:7, :] = recip
    stage = 1 + ITERS
    to_group(lambda i: fields.at[peers[i][0]], lambda i: field_inbox.at[i], stage)
    held = fields[me]
    all_of(arrived, halo_send, halo_recv).wait_send()
    all_of(others, group_send.at[0], group_recv.at[0]).wait_send()
    all_of(starts, group_send.at[1], group_recv.at[1]).wait_send()
    for sent in range(ITERS):
        ring_stage(sent, 0).wait_send()
        ring_stage(sent, 1).wait_send()
        if sent < turn:
            post_stage(sent).wait_send()
    all_of(field_inbox, group_send.at[stage], group_recv.at[stage]).wait()
    for i in range(group - 1):
        held = held + field_inbox[i]
    fields[me] = held
    step = norm / (stiff_part + scale * fields[me, 6:7, :])
    vectors[2] = vectors[2] + step * vectors[1]
    charges = vectors[2, pl.ds(me, 1), :]
    charges_ref[...] = charges
    for axis in range(3):
        field = fields[me, axis : axis + 1, :] + step * fields[me, 3 + axis : 4 + axis, :]
        forces_ref[axis] = charges * (scale * field)


def shards(
    equivariant_embedding,
    cartesian_coordinates,
    element_identity,
    occupied_site_totals,
    halo_export_indices,
    adjacency_rows,
    attention_source_weights,
    attention_target_weights,
    degree_channel_mixer,
    affinity_output_head,
    baseline_affinity_per_element,
    chemical_stiffness,
    reciprocal_lattice_points,
    ewald_weighting,
):
    chips_x = CHIPS_X
    ring = lax.axis_size("slab") // 2
    shape = (chips_x, ring, lax.axis_size("dom") // chips_x)
    assert shape[1] == shape[2]
    comps = equivariant_embedding.shape[3]
    ghosts = halo_export_indices.shape[2]
    degrees = degree_channel_mixer.shape[0]
    lists = adjacency_rows.shape[3]
    elements = chemical_stiffness.shape[0]
    group = 2 * chips_x
    blocks = reciprocal_lattice_points.shape[1] // LANES // group
    rows = 2 * blocks + 1
    table_size = LANES + 8 * ghosts
    bf16, i32 = jnp.bfloat16, jnp.int32
    assert group * TILE <= LANES and comps + 1 == sum(CHUNKS[-1])
    vmem = pl.BlockSpec(memory_space=pltpu.VMEM)
    smem = pl.BlockSpec(memory_space=pltpu.SMEM)
    hbm = pl.BlockSpec(memory_space=pltpu.HBM)
    dma = pltpu.SemaphoreType.DMA
    operands = (
        jnp.transpose(equivariant_embedding[0, 0], (1, 0, 2)),
        degree_channel_mixer,
        attention_source_weights,
        attention_target_weights,
        halo_export_indices[0],
        cartesian_coordinates[0, 0].reshape(3, 1, LANES),
        element_identity[0],
        adjacency_rows[0, 0].T,
        affinity_output_head,
        ewald_weighting.reshape(group, blocks, LANES),
        reciprocal_lattice_points,
        baseline_affinity_per_element.reshape(1, elements),
        chemical_stiffness.reshape(1, elements),
    )
    charges, forces = pl.pallas_call(
        lambda *refs: whole_kernel(shape, *refs),
        name="equilibrate",
        out_shape=(
            jax.ShapeDtypeStruct((1, LANES), F32),
            jax.ShapeDtypeStruct((3, 1, LANES), F32),
        ),
        in_specs=[hbm] * 13 + [smem],
        out_specs=(vmem, vmem),
        scratch_shapes=[
            pltpu.VMEM((comps, LANES, LANES), bf16),
            pltpu.VMEM((degrees, LANES, LANES), bf16),
            pltpu.VMEM((LANES, LANES), bf16),
            pltpu.VMEM((LANES, LANES), bf16),
            pltpu.VMEM((1, ghosts), i32),
            pltpu.VMEM((3, 1, LANES), F32),
            pltpu.VMEM((1, LANES), i32),
            pltpu.VMEM((lists, LANES), i32),
            pltpu.VMEM((degrees, LANES), F32),
            pltpu.VMEM((group, blocks, LANES), F32),
            pltpu.VMEM((3, blocks * LANES), F32),
            pltpu.VMEM((1, elements), F32),
            pltpu.VMEM((1, elements), F32),
            pltpu.VMEM((LANES, LANES), bf16),
            pltpu.VMEM((comps + 1, LANES, LANES), bf16),
            pltpu.VMEM((comps + 1, ghosts, LANES), bf16),
            pltpu.VMEM((comps + 1, 8, ghosts, LANES), bf16),
            pltpu.VMEM((table_size, LANES), F32),
            pltpu.VMEM((LANES, table_size), F32),
            pltpu.VMEM((comps, LANES, LANES), F32),
            pltpu.VMEM((group * blocks, LANES, LANES), F32),
            pltpu.VMEM((group * blocks, LANES, LANES), F32),
            pltpu.VMEM((3, LANES, LANES), F32),
            pltpu.VMEM((group, TILE, LANES), F32),
            pltpu.VMEM((group, 1, LANES), F32),
            pltpu.VMEM((5, group, LANES), F32),
            pltpu.VMEM((ITERS, 2, rows, LANES), F32),
            pltpu.VMEM((ITERS, 2, ring - 1, rows, LANES), F32),
            pltpu.VMEM((rows, LANES), F32),
            pltpu.VMEM((6, blocks, LANES), F32),
            pltpu.VMEM((ITERS - 1, group + 1, LANES), F32),
            pltpu.VMEM((ITERS - 1, group - 1, group + 1, LANES), F32),
            pltpu.VMEM((group + 1, LANES), F32),
            pltpu.VMEM((LANES, LANES), F32),
            pltpu.VMEM((group, TILE, LANES), F32),
            pltpu.VMEM((group - 1, TILE, LANES), F32),
            dma((13,)),
            dma,
            dma,
            dma((len(CHUNKS), 3)),
            dma((ITERS + 2,)),
            dma((ITERS + 2,)),
            dma((ITERS, 2)),
            dma((ITERS, 2)),
        ],
        compiler_params=pltpu.CompilerParams(
            collective_id=1, has_side_effects=True, vmem_limit_bytes=48 * 1024 * 1024
        ),
    )(*(pltpu.with_memory_space_constraint(item, pltpu.HBM) for item in operands), occupied_site_totals)
    return (charges.reshape(1, 1, LANES), forces.reshape(1, 1, 3, LANES))


def solution(mesh):
    placed = (
        P("dom", "slab", None, None, None),
        P("dom", "slab", None, None),
        P("dom", "slab", None),
        P("dom", "slab"),
        P("dom", "slab", None),
        P("dom", "slab", None, None),
        P(),
        P(),
        P(),
        P(),
        P(),
        P(),
        P(),
        P(),
    )
    return jax.shard_map(
        shards,
        mesh=mesh,
        in_specs=placed,
        out_specs=(P("dom", "slab", None), P("dom", "slab", None, None)),
        check_vma=False,
    )
```

```python
import math

import jax
import jax.numpy as jnp
from jax import lax
from jax.experimental import pallas as pl
from jax.experimental.pallas import tpu as pltpu
from jax.sharding import PartitionSpec as P

ITERS = 4
CHIPS_X = 4
LANES = 128
MESH = pl.DeviceIdType.MESH
F32 = jnp.float32

HALF_PI_PARTS = (1.57080078125, math.pi / 2 - 1.57080078125)


def sine_cosine(phase):
    quadrant = jnp.round(phase * (2.0 / math.pi))
    reduced = phase - quadrant * HALF_PI_PARTS[0]
    reduced = reduced - quadrant * HALF_PI_PARTS[1]
    square = reduced * reduced
    odd = (-1.9515295891e-4 * square + 8.3321608736e-3) * square - 1.6666654611e-1
    odd = odd * square * reduced + reduced
    even = (2.443315711809948e-5 * square - 1.388731625493765e-3) * square
    even = (even + 4.166664568298827e-2) * square * square - 0.5 * square + 1.0
    turn = quadrant.astype(jnp.int32)
    swap = (turn & 1) == 1
    sine = jnp.where(swap, even, odd)
    cosine = jnp.where(swap, odd, even)
    sine = jnp.where((turn & 2) == 2, -sine, sine)
    cosine = jnp.where(((turn + 1) & 2) == 2, -cosine, cosine)
    return sine, cosine


CHUNKS = ((0, 13), (13, 8), (21, 5))
BLOCKS = (1, 7, 3, 5, 0, 2, 6, 8)
SCALARS = 3
TILE = 8


def place_of(shape):
    chips_x, chips_y, chips_z = shape
    dom, slab = lax.axis_index("dom"), lax.axis_index("slab")
    return lax.div(dom, chips_z), lax.div(slab, 2), lax.rem(dom, chips_z), lax.rem(slab, 2)


def device(shape, x, y, z, core):
    return (x * shape[2] + z, y * 2 + core)


def far_first(count):
    return sorted(range(1, count), key=lambda j: -min(j, count - j))


def sum_partners(shape):
    x, y, z, core = place_of(shape)
    chips_x, ring, _ = shape
    mine = x * 2 + core
    peers = []
    steps = [(dx, dc) for dx in far_first(chips_x) for dc in (0, 1)] + [(0, 1)]
    for dx, dc in steps:
        other_x, other_core = lax.rem(x + dx, chips_x), lax.rem(core + dc, 2)
        peers.append((other_x * 2 + other_core, device(shape, other_x, y, z, other_core)))
    along = [
        device(shape, x, lax.rem(y + j * (1 - core), ring), lax.rem(z + j * core, ring), core)
        for j in far_first(ring)
    ]
    across = [
        device(shape, x, lax.rem(y + j * core, ring), lax.rem(z + j * (1 - core), ring), core)
        for j in far_first(ring)
    ]
    return mine, peers, along, across


def halo_partners(shape):
    x, y, z, core = place_of(shape)
    domains = shape[0] * shape[2]
    dom, slab = lax.axis_index("dom"), lax.axis_index("slab")
    way = 1 - 2 * core
    return {
        "before": (lax.rem(dom + domains - 1, domains), slab),
        "after": (lax.rem(dom + 1, domains), slab),
        "pair": (dom, y * 2 + 1 - core),
        "outer": (dom, lax.rem(slab + 2 * shape[1] - way, 2 * shape[1])),
        "ahead": (lax.rem(dom + domains + way, domains), slab),
    }


def row_of(column, eye):
    return jnp.sum(jnp.where(eye, column, 0.0), axis=0, keepdims=True)


def identity_mask(count):
    shape = (count, count)
    return lax.broadcasted_iota(jnp.int32, shape, 0) == lax.broadcasted_iota(jnp.int32, shape, 1)


def degrees_of(comps):
    return [range(l * l, (l + 1) * (l + 1)) for l in range(math.isqrt(comps))]


def fill_mask(adjacency_ref, upright, mask_ref):
    size = upright.shape[0]
    ghosts = (size - LANES) // 8
    group = 64

    def per_group(part, carry):
        start = part * group
        row = lax.broadcasted_iota(jnp.int32, (group, LANES), 0) + start
        slot = row - LANES
        shift = jnp.zeros_like(row)
        for i, block in enumerate(BLOCKS):
            inside = (slot >= i * ghosts) & (slot < (i + 1) * ghosts)
            shift = jnp.where(inside, (block - i) * ghosts, shift)
        row = row + shift
        hit = row == adjacency_ref[0:1, :]
        for j in range(1, adjacency_ref.shape[0]):
            hit = hit | (row == adjacency_ref[j : j + 1, :])
        upright[pl.ds(pl.multiple_of(start, group), group), :] = jnp.where(hit, 1.0, 0.0)
        return carry

    lax.fori_loop(0, size // group, per_group, 0)
    for part in range(size // LANES):
        span = slice(part * LANES, (part + 1) * LANES)
        mask_ref[:, span] = upright[span, :].T


def attention(queries, keys, mask):
    scores = lax.dot_general(
        queries, keys, (((1,), (1,)), ((), ())), preferred_element_type=F32
    )
    gate = jax.nn.sigmoid(scores / math.sqrt(LANES)) * 0.125
    return jnp.where(mask > 0.0, gate, 0.0).astype(jnp.bfloat16)


def spread(rows):
    return jnp.concatenate([rows] * (LANES // rows.shape[0]), axis=0).T


def wide(columns, index):
    return jnp.broadcast_to(columns[:, index : index + 1], (LANES, LANES))


def fill_tables(first, stop, blocks, waves, about, sites, cos_ref, sin_ref):
    step_rows = 64

    def per_member(member, carry):
        columns = spread(about[member])
        for axis in range(3):
            sites[axis] = wide(columns, axis)

        def per_rows(part, inner):
            block, rows = part // (LANES // step_rows), part % (LANES // step_rows)
            lanes = pl.ds(pl.multiple_of(block * LANES, LANES), LANES)
            rows = pl.ds(pl.multiple_of(rows * step_rows, step_rows), step_rows)
            phase = (
                sites[0, rows, :] * waves[0:1, lanes]
                + sites[1, rows, :] * waves[1:2, lanes]
                + sites[2, rows, :] * waves[2:3, lanes]
            )
            sine, cosine = sine_cosine(phase)
            cos_ref[member * blocks + block, rows, :] = cosine
            sin_ref[member * blocks + block, rows, :] = sine
            return inner

        return lax.fori_loop(0, blocks * LANES // step_rows, per_rows, carry)

    lax.fori_loop(first, stop, per_member, 0)


def whole_kernel(
    shape,
    features_hbm,
    mixer_hbm,
    source_hbm,
    target_hbm,
    export_hbm,
    place_hbm,
    species_hbm,
    adjacency_hbm,
    head_hbm,
    weight_hbm,
    waves_hbm,
    baseline_hbm,
    stiffness_hbm,
    count_ref,
    charges_ref,
    forces_ref,
    features_ref,
    mixer_ref,
    source_ref,
    target_ref,
    export_ref,
    place_ref,
    species_ref,
    adjacency_ref,
    head_ref,
    weight_ref,
    waves,
    baseline_ref,
    stiffness_ref,
    queries,
    table,
    outgoing,
    arrived,
    upright,
    mask_ref,
    own_message,
    cos_ref,
    sin_ref,
    sites,
    about,
    first_rows,
    vectors,
    parts,
    inbox,
    ring_total,
    factors,
    posts,
    post_inbox,
    post_total,
    matrix,
    fields,
    field_inbox,
    load_sem,
    halo_send,
    halo_recv,
    near_recv,
    group_send,
    group_recv,
    ring_send,
    ring_recv,
):
    me, peers, along, across = sum_partners(shape)
    near = halo_partners(shape)
    core = place_of(shape)[3]
    group = len(peers) + 1
    comps = features_ref.shape[0]
    ghosts = outgoing.shape[1]
    blocks = cos_ref.shape[0] // group
    span = blocks * LANES
    scale = 1.0 / math.sqrt(lax.axis_size("dom") * lax.axis_size("slab") * LANES)
    bf16 = jnp.bfloat16

    own_waves = waves_hbm.at[:, pl.ds(pl.multiple_of(me * span, LANES), span)]
    loads = [
        pltpu.make_async_copy(source, target, load_sem.at[i])
        for i, (source, target) in enumerate(
            (
                (features_hbm, features_ref),
                (mixer_hbm, mixer_ref),
                (source_hbm, source_ref),
                (target_hbm, target_ref),
                (export_hbm, export_ref),
                (place_hbm, place_ref),
                (species_hbm, species_ref),
                (adjacency_hbm, adjacency_ref),
                (head_hbm, head_ref),
                (weight_hbm, weight_ref),
                (own_waves, waves),
                (baseline_hbm, baseline_ref),
                (stiffness_hbm, stiffness_ref),
            )
        )
    ]
    for item in loads:
        item.start()
    everyone = [near[name] for name in ("before", "after", "pair", "outer")]
    everyone += [peer for _, peer in peers] + along + across
    barrier = pltpu.get_barrier_semaphore()
    for partner in everyone:
        pl.semaphore_signal(barrier, inc=1, device_id=partner, device_id_type=MESH)
    eye = identity_mask(LANES)

    for i in (5, 6, 11, 12):
        loads[i].wait()
    species = species_ref[...]
    hardness = jnp.zeros(species.shape, F32)
    baseline = jnp.zeros(species.shape, F32)
    for element in range(stiffness_ref.shape[1]):
        here = species == element
        hardness = jnp.where(here, stiffness_ref[0:1, element : element + 1], hardness)
        baseline = jnp.where(here, baseline_ref[0:1, element : element + 1], baseline)
    live = lax.broadcasted_iota(jnp.int32, (1, LANES), 1) < count_ref[0, 0]
    live = jnp.where(live, 1.0, 0.0)
    about[me] = jnp.zeros((TILE, LANES), F32)
    for axis in range(3):
        about[me, axis : axis + 1, :] = place_ref[axis]
    about[me, 3:4, :] = hardness
    about[me, 4:5, :] = live

    for i in range(5):
        loads[i].wait()
    offered = jnp.broadcast_to(export_ref[...], (ghosts, ghosts)).astype(F32)
    offered = jnp.sum(jnp.where(identity_mask(ghosts), offered, 0.0), axis=1, keepdims=True)
    slots = lax.broadcasted_iota(jnp.int32, (ghosts, LANES), 1).astype(F32)
    pick = jnp.where(slots == offered, 1.0, 0.0).astype(bf16)
    def offer(chunk):
        for index in range(CHUNKS[chunk][0], sum(CHUNKS[chunk])):
            comp = 0 if index == comps else index
            mix = target_ref[...] if index == comps else mixer_ref[math.isqrt(comp)]
            row = jnp.dot(pick, features_ref[comp], preferred_element_type=F32).astype(bf16)
            outgoing[index] = jnp.dot(row, mix, preferred_element_type=F32).astype(bf16)

    pl.semaphore_wait(barrier, len(everyone))

    def ship(chunk, source, slot, target, sem):
        rows = pl.ds(*CHUNKS[chunk])
        copy = pltpu.make_async_remote_copy(
            src_ref=source,
            dst_ref=arrived.at[rows, slot],
            send_sem=halo_send,
            recv_sem=sem,
            device_id=target,
            device_id_type=MESH,
        )
        copy.start()

    def own(chunk):
        return outgoing.at[pl.ds(*CHUNKS[chunk])]

    def got(chunk, slot):
        return arrived.at[pl.ds(*CHUNKS[chunk]), slot]

    def all_of(ref, send, receive):
        return pltpu.make_async_remote_copy(
            src_ref=ref,
            dst_ref=ref,
            send_sem=send,
            recv_sem=receive,
            device_id=near["pair"],
            device_id_type=MESH,
        )

    def to_group(pieces, drops, stage):
        for i, (_, target) in enumerate(peers):
            pltpu.make_async_remote_copy(
                src_ref=pieces(i),
                dst_ref=drops(i),
                send_sem=group_send.at[stage],
                recv_sem=group_recv.at[stage],
                device_id=target,
                device_id_type=MESH,
            ).start()

    to_group(lambda i: about.at[me], lambda i: about.at[me], 0)
    for chunk in range(len(CHUNKS)):
        offer(chunk)
        ship(chunk, own(chunk), 0, near["after"], near_recv.at[chunk, 0])
        ship(chunk, own(chunk), 1, near["before"], near_recv.at[chunk, 0])
        ship(chunk, own(chunk), 3 - core, near["outer"], near_recv.at[chunk, 1])
        ship(chunk, own(chunk), 2 + core, near["pair"], near_recv.at[chunk, 2])

    def relay_outer(chunk):
        all_of(got(chunk, 0), halo_send, near_recv.at[chunk, 1]).wait_recv()
        ship(chunk, got(chunk, 2 + core), 4 + 3 * core, near["ahead"], halo_recv)

    def relay_near(chunk):
        both = arrived.at[pl.ds(*CHUNKS[chunk]), pl.ds(0, 2)]
        all_of(both, halo_send, near_recv.at[chunk, 0]).wait_recv()
        ship(chunk, got(chunk, core), 5 + core, near["outer"], halo_recv)
        ship(chunk, got(chunk, 0), 4 + core, near["pair"], halo_recv)
        ship(chunk, got(chunk, 1), 6 + core, near["pair"], halo_recv)

    def tables_of(first, stop):
        fill_tables(first, stop, blocks, waves, about, sites, cos_ref, sin_ref)

    loads[7].wait()
    fill_mask(adjacency_ref, upright, mask_ref)
    relay_outer(0)
    for degree, members in enumerate(degrees_of(comps)):
        for comp in members:
            product = jnp.dot(
                features_ref[comp], mixer_ref[degree], preferred_element_type=F32
            )
            table[comp] = product.astype(bf16)
    scalar = features_ref[0]
    table[comps] = jnp.dot(scalar, target_ref[...], preferred_element_type=F32).astype(bf16)
    queries[...] = jnp.dot(scalar, source_ref[...], preferred_element_type=F32).astype(bf16)
    for i in range(8, 11):
        loads[i].wait()
    others = about.at[pl.ds(0, group - 1)]
    all_of(others, group_send.at[0], group_recv.at[0]).wait_recv()
    tables_of(0, group // 4)
    relay_near(0)
    relay_outer(1)
    tables_of(group // 4, group // 2)
    relay_near(1)
    relay_outer(2)
    tables_of(group // 2, 5 * group // 8)
    relay_near(2)
    for chunk in range(len(CHUNKS)):
        all_of(got(chunk, 0), halo_send, near_recv.at[chunk, 2]).wait_recv()

    def both_of(comp):
        return jnp.concatenate([table[comp], arrived[comp, 0:4].reshape(4 * ghosts, LANES)], axis=0)

    reach = LANES + 4 * ghosts
    near_weights = attention(queries[...], both_of(comps), mask_ref[:, 0:reach])
    for comp in range(comps):
        own_message[comp] = jnp.dot(near_weights, both_of(comp), preferred_element_type=F32)
    tables_of(5 * group // 8, group)
    for member in range(group):
        vectors[3, member : member + 1, :] = about[member, 3:4, :]
        vectors[4, member : member + 1, :] = about[member, 4:5, :]
    vectors[1] = jnp.zeros((group, LANES), F32)
    vectors[2] = jnp.zeros((group, LANES), F32)
    factors[...] = jnp.zeros_like(factors)
    all_of(arrived.at[:, pl.ds(0, 4)], halo_send, halo_recv).wait_recv()

    far_keys = arrived[comps, 4:8].reshape(4 * ghosts, LANES)
    weights = attention(queries[...], far_keys, mask_ref[:, reach:])
    readout = jnp.zeros((LANES, LANES), F32)
    for degree, members in enumerate(degrees_of(comps)):
        square = jnp.zeros((LANES, LANES), F32)
        for comp in members:
            message = own_message[comp] + jnp.dot(
                weights, arrived[comp, 4:8].reshape(4 * ghosts, LANES), preferred_element_type=F32
            )
            square = message if degree == 0 else square + message * message
        norm = square if degree == 0 else jnp.sqrt(square + 1e-06)
        readout = readout + norm * head_ref[degree : degree + 1, :]
    electroneg = row_of(jnp.sum(readout, axis=1, keepdims=True), eye) + baseline
    first_rows[me] = -electroneg * live
    to_group(lambda i: first_rows.at[me], lambda i: first_rows.at[me], 1)
    starts = first_rows.at[pl.ds(0, group - 1)]
    all_of(starts, group_send.at[1], group_recv.at[1]).wait_recv()
    for member in range(group):
        vectors[0, member : member + 1, :] = first_rows[member]

    lanes = lax.broadcasted_iota(jnp.int32, (LANES, LANES), 1)
    scalar_row = 2 * blocks
    weight = weight_ref[me]
    tables = (cos_ref, sin_ref)

    def full_sum(rows):
        return jnp.sum(jnp.sum(rows, axis=0, keepdims=True), axis=1, keepdims=True)

    def project(turn):
        residual = vectors[0]
        columns = spread(residual)
        sums = [[jnp.zeros((TILE, LANES), F32) for _ in range(blocks)] for _ in range(2)]
        for member in range(group):
            column = wide(columns, member)
            for part in range(2):
                for block in range(blocks):
                    product = tables[part][member * blocks + block] * column
                    product = product.reshape(LANES // TILE, TILE, LANES)
                    sums[part][block] = sums[part][block] + jnp.sum(product, axis=0)
        for part in range(2):
            for block in range(blocks):
                row = part * blocks + block
                parts[turn, 0, row : row + 1, :] = jnp.sum(
                    sums[part][block], axis=0, keepdims=True
                )
        hard_residual = vectors[3] * residual
        scalars = (residual * residual, hard_residual * residual, hard_residual * vectors[1])
        row = jnp.zeros((1, LANES), F32)
        for i, product in enumerate(scalars):
            row = jnp.where(lanes[0:1, :] == i, full_sum(product), row)
        parts[turn, 0, scalar_row : scalar_row + 1, :] = row

    def ring_stage(turn, stage):
        sems = (ring_send.at[turn, stage], ring_recv.at[turn, stage])
        return all_of(inbox.at[turn, stage], *sems)

    def post_stage(turn):
        return all_of(post_inbox.at[turn], group_send.at[2 + turn], group_recv.at[2 + turn])

    def ring_sum(turn, meanwhile):
        held = parts[turn, 0]
        for stage, targets in enumerate((along, across)):
            if stage > 0:
                parts[turn, stage] = held
            for i, target in enumerate(targets):
                pltpu.make_async_remote_copy(
                    src_ref=parts.at[turn, stage],
                    dst_ref=inbox.at[turn, stage, i],
                    send_sem=ring_send.at[turn, stage],
                    recv_sem=ring_recv.at[turn, stage],
                    device_id=target,
                    device_id_type=MESH,
                ).start()
            if stage == 0:
                meanwhile()
            ring_stage(turn, stage).wait_recv()
            for i in range(len(targets)):
                held = held + inbox[turn, stage, i]
        ring_total[...] = held

    def follow(turn, previous_norm, stiff_part):
        norm, pure, mixed = (
            jnp.broadcast_to(ring_total[scalar_row : scalar_row + 1, i : i + 1], (1, LANES))
            for i in range(SCALARS)
        )
        beta = jnp.where(turn > 0, norm / previous_norm, 0.0)
        stiff_part = pure + 2.0 * beta * mixed + beta * beta * stiff_part
        recip = jnp.zeros_like(weight)
        for part in range(2):
            rows = ring_total[part * blocks : (part + 1) * blocks, :] + beta * factors[part]
            factors[part] = rows
            factors[2 + part] = weight * rows
            recip = recip + weight * rows * rows
        vectors[1] = vectors[0] + beta * vectors[1]
        return norm, stiff_part, jnp.broadcast_to(full_sum(recip), (1, LANES))

    def iteration(turn, carry):
        project(turn)
        ring_sum(turn, lambda: None)
        norm, stiff_part, recip = follow(turn, *carry)

        def back(step, acc):
            for j in range(4):
                member = 4 * step + j
                image = jnp.zeros((LANES, LANES), F32)
                for block in range(blocks):
                    for part in range(2):
                        row = factors[2 + part, block : block + 1, :]
                        image = image + tables[part][member * blocks + block] * row
                acc = jnp.where(lanes == member, jnp.sum(image, axis=1, keepdims=True), acc)
            return acc

        images = lax.fori_loop(0, group // 4, back, jnp.zeros((LANES, LANES), F32))
        posts[turn, 0:group, :] = images.T[0:group, :]
        posts[turn, group : group + 1, :] = recip
        to_group(lambda i: posts.at[turn], lambda i: post_inbox.at[turn, i], 2 + turn)
        held = posts[turn]
        post_stage(turn).wait_recv()
        for i in range(group - 1):
            held = held + post_inbox[turn, i]
        post_total[...] = held
        step = norm / (stiff_part + scale * post_total[group : group + 1, :])
        direction = vectors[1]
        image = vectors[4] * (vectors[3] * direction + scale * post_total[0:group, :])
        vectors[2] = vectors[2] + step * direction
        vectors[0] = vectors[0] - step * image
        for part in range(2):
            factors[4 + part] = factors[4 + part] + step * factors[2 + part]
        return norm, stiff_part

    def field_of(first, offset):
        half = LANES // 2

        def per_pair(step, carry):
            for part in range(4):
                member = 2 * step + part // 2
                rows = pl.ds(part % 2 * half, half)
                sums = [jnp.zeros((half, LANES), F32) for _ in range(3)]
                for block in range(blocks):
                    where = member * blocks + block
                    term = (
                        sin_ref[where, rows, :] * factors[first, block : block + 1, :]
                        - cos_ref[where, rows, :] * factors[first + 1, block : block + 1, :]
                    )
                    for axis in range(3):
                        wave = waves[axis : axis + 1, block * LANES : (block + 1) * LANES]
                        sums[axis] = sums[axis] + term * wave
                filled = matrix[rows, :]
                for axis in range(3):
                    column = jnp.sum(sums[axis], axis=1, keepdims=True)
                    place = member * TILE + offset + axis
                    filled = jnp.where(lanes[0:half, :] == place, column, filled)
                matrix[rows, :] = filled
            return carry

        lax.fori_loop(0, group // 2, per_pair, 0)

    ones = jnp.ones((1, LANES), F32)
    carry = lax.fori_loop(0, ITERS - 1, iteration, (ones, ones))

    turn = ITERS - 1
    matrix[...] = jnp.zeros_like(matrix)
    project(turn)
    ring_sum(turn, lambda: field_of(4, 0))
    norm, stiff_part, recip = follow(turn, *carry)
    field_of(2, 3)
    field_rows = matrix[...].T
    for member in range(group):
        fields[member] = field_rows[member * TILE : (member + 1) * TILE, :]
        fields[member, 6:7, :] = recip
    stage = 1 + ITERS
    to_group(lambda i: fields.at[peers[i][0]], lambda i: field_inbox.at[i], stage)
    held = fields[me]
    all_of(arrived, halo_send, halo_recv).wait_send()
    all_of(others, group_send.at[0], group_recv.at[0]).wait_send()
    all_of(starts, group_send.at[1], group_recv.at[1]).wait_send()
    for sent in range(ITERS):
        ring_stage(sent, 0).wait_send()
        ring_stage(sent, 1).wait_send()
        if sent < turn:
            post_stage(sent).wait_send()
    all_of(field_inbox, group_send.at[stage], group_recv.at[stage]).wait()
    for i in range(group - 1):
        held = held + field_inbox[i]
    fields[me] = held
    step = norm / (stiff_part + scale * fields[me, 6:7, :])
    vectors[2] = vectors[2] + step * vectors[1]
    charges = vectors[2, pl.ds(me, 1), :]
    charges_ref[...] = charges
    for axis in range(3):
        field = fields[me, axis : axis + 1, :] + step * fields[me, 3 + axis : 4 + axis, :]
        forces_ref[axis] = charges * (scale * field)


def hand_over(charges_ref, forces_ref, charges_out, forces_out):
    charges_out[...] = charges_ref[...]
    forces_out[...] = forces_ref[...]


def shards(
    equivariant_embedding,
    cartesian_coordinates,
    element_identity,
    occupied_site_totals,
    halo_export_indices,
    adjacency_rows,
    attention_source_weights,
    attention_target_weights,
    degree_channel_mixer,
    affinity_output_head,
    baseline_affinity_per_element,
    chemical_stiffness,
    reciprocal_lattice_points,
    ewald_weighting,
):
    chips_x = CHIPS_X
    ring = lax.axis_size("slab") // 2
    shape = (chips_x, ring, lax.axis_size("dom") // chips_x)
    assert shape[1] == shape[2]
    comps = equivariant_embedding.shape[3]
    ghosts = halo_export_indices.shape[2]
    degrees = degree_channel_mixer.shape[0]
    lists = adjacency_rows.shape[3]
    elements = chemical_stiffness.shape[0]
    group = 2 * chips_x
    blocks = reciprocal_lattice_points.shape[1] // LANES // group
    rows = 2 * blocks + 1
    table_size = LANES + 8 * ghosts
    bf16, i32 = jnp.bfloat16, jnp.int32
    assert group * TILE <= LANES and comps + 1 == sum(CHUNKS[-1])
    vmem = pl.BlockSpec(memory_space=pltpu.VMEM)
    smem = pl.BlockSpec(memory_space=pltpu.SMEM)
    hbm = pl.BlockSpec(memory_space=pltpu.HBM)
    dma = pltpu.SemaphoreType.DMA
    operands = (
        jnp.transpose(equivariant_embedding[0, 0], (1, 0, 2)),
        degree_channel_mixer,
        attention_source_weights,
        attention_target_weights,
        halo_export_indices[0],
        cartesian_coordinates[0, 0].reshape(3, 1, LANES),
        element_identity[0],
        adjacency_rows[0, 0].T,
        affinity_output_head,
        ewald_weighting.reshape(group, blocks, LANES),
        reciprocal_lattice_points,
        baseline_affinity_per_element.reshape(1, elements),
        chemical_stiffness.reshape(1, elements),
    )
    charges, forces = pl.pallas_call(
        lambda *refs: whole_kernel(shape, *refs),
        name="equilibrate",
        out_shape=(
            jax.ShapeDtypeStruct((1, LANES), F32),
            jax.ShapeDtypeStruct((3, 1, LANES), F32),
        ),
        in_specs=[hbm] * 13 + [smem],
        out_specs=(vmem, vmem),
        scratch_shapes=[
            pltpu.VMEM((comps, LANES, LANES), bf16),
            pltpu.VMEM((degrees, LANES, LANES), bf16),
            pltpu.VMEM((LANES, LANES), bf16),
            pltpu.VMEM((LANES, LANES), bf16),
            pltpu.VMEM((1, ghosts), i32),
            pltpu.VMEM((3, 1, LANES), F32),
            pltpu.VMEM((1, LANES), i32),
            pltpu.VMEM((lists, LANES), i32),
            pltpu.VMEM((degrees, LANES), F32),
            pltpu.VMEM((group, blocks, LANES), F32),
            pltpu.VMEM((3, blocks * LANES), F32),
            pltpu.VMEM((1, elements), F32),
            pltpu.VMEM((1, elements), F32),
            pltpu.VMEM((LANES, LANES), bf16),
            pltpu.VMEM((comps + 1, LANES, LANES), bf16),
            pltpu.VMEM((comps + 1, ghosts, LANES), bf16),
            pltpu.VMEM((comps + 1, 8, ghosts, LANES), bf16),
            pltpu.VMEM((table_size, LANES), F32),
            pltpu.VMEM((LANES, table_size), F32),
            pltpu.VMEM((comps, LANES, LANES), F32),
            pltpu.VMEM((group * blocks, LANES, LANES), F32),
            pltpu.VMEM((group * blocks, LANES, LANES), F32),
            pltpu.VMEM((3, LANES, LANES), F32),
            pltpu.VMEM((group, TILE, LANES), F32),
            pltpu.VMEM((group, 1, LANES), F32),
            pltpu.VMEM((5, group, LANES), F32),
            pltpu.VMEM((ITERS, 2, rows, LANES), F32),
            pltpu.VMEM((ITERS, 2, ring - 1, rows, LANES), F32),
            pltpu.VMEM((rows, LANES), F32),
            pltpu.VMEM((6, blocks, LANES), F32),
            pltpu.VMEM((ITERS - 1, group + 1, LANES), F32),
            pltpu.VMEM((ITERS - 1, group - 1, group + 1, LANES), F32),
            pltpu.VMEM((group + 1, LANES), F32),
            pltpu.VMEM((LANES, LANES), F32),
            pltpu.VMEM((group, TILE, LANES), F32),
            pltpu.VMEM((group - 1, TILE, LANES), F32),
            dma((13,)),
            dma,
            dma,
            dma((len(CHUNKS), 3)),
            dma((ITERS + 2,)),
            dma((ITERS + 2,)),
            dma((ITERS, 2)),
            dma((ITERS, 2)),
        ],
        compiler_params=pltpu.CompilerParams(
            collective_id=1, has_side_effects=True, vmem_limit_bytes=48 * 1024 * 1024
        ),
    )(*(pltpu.with_memory_space_constraint(item, pltpu.HBM) for item in operands), occupied_site_totals)
    charges, forces = pl.pallas_call(
        hand_over,
        name="results",
        out_shape=(
            jax.ShapeDtypeStruct((1, LANES), F32),
            jax.ShapeDtypeStruct((3, 1, LANES), F32),
        ),
        in_specs=[vmem, vmem],
        out_specs=(vmem, vmem),
        compiler_params=pltpu.CompilerParams(vmem_limit_bytes=1024 * 1024),
    )(charges, forces)
    return (charges.reshape(1, 1, LANES), forces.reshape(1, 1, 3, LANES))


def solution(mesh):
    placed = (
        P("dom", "slab", None, None, None),
        P("dom", "slab", None, None),
        P("dom", "slab", None),
        P("dom", "slab"),
        P("dom", "slab", None),
        P("dom", "slab", None, None),
        P(),
        P(),
        P(),
        P(),
        P(),
        P(),
        P(),
        P(),
    )
    return jax.shard_map(
        shards,
        mesh=mesh,
        in_specs=placed,
        out_specs=(P("dom", "slab", None), P("dom", "slab", None, None)),
        check_vma=False,
    )
```
